512 devices in a mesh: elem: 64 (over x, z_hi, y, core), lev: 8 (over z_lo).
Axes of the slice: x: 4, y: 4, z: 16 (z_hi: 2, z_lo: 8; z = z_hi * 8 + z_lo), core: 2. Of those that a mesh axis runs over, the one named last changes fastest.
Arguments:
- zonal_wind: float32 [128, 16, 8192], P('lev', None, 'elem'), may hold values from -6 to 6
- meridional_wind: float32 [128, 16, 8192], P('lev', None, 'elem'), may hold values from -6 to 6
- vertical_wind: float32 [128, 16, 8192], P('lev', None, 'elem'), may hold values from -6 to 6
- pressure: float32 [128, 16, 8192], P('lev', None, 'elem'), may hold values from -6 to 6
- geopotential: float32 [128, 16, 8192], P('lev', None, 'elem'), may hold values from -6 to 6
- layer_mass: float32 [128, 16, 8192], P('lev', None, 'elem'), may hold values from 0.5 to 2
- stiffness: float32 [128, 16, 8192], P(None, 'lev', 'elem'), may hold values from 4 to 1024
- elem_order: int32 [64, 128], P('elem'), may hold values from 0 to 127, each once within a row
Outputs:
- zonal_out: float32 [128, 16, 8192], P('lev', None, 'elem')
- meridional_out: float32 [128, 16, 8192], P('lev', None, 'elem')
- vertical_out: float32 [128, 16, 8192], P('lev', None, 'elem')
- pressure_out: float32 [128, 16, 8192], P('lev', None, 'elem')
- geopotential_out: float32 [128, 16, 8192], P('lev', None, 'elem')
The draws below stay inside these ranges and needn't reach their ends.
Inputs may be any that keep to these rules, and one draw needn't show every extreme that they name: `elem_order`: each row is a permutation of the positions 0 .. 127 of its strip.
All inputs are finite; a program needn't handle non-finite values.
Results may differ from the reference program's by a relative error of at most 0.0003.
Values sent between devices are 32-bit elements; how exact they have to be, the bound alone decides.
No kernel may reach another device: no remote copies, remote signals or barrier semaphores. Data moves between devices by JAX's collectives and lax.ppermute only.
A program may use at most 128 MiB of HBM per device.

```python
import math
import jax
import jax.numpy as jnp
import numpy as np
from jax import lax

NLEV = 128
NODES = 16
SUBSTEPS = 3
EY = 128
STRIPS = 64
NELEM = 8192


def steps_of(own_key, dims, pieces, smallest, top_value):
    def one(position, shards_of):
        draws = jax.random.uniform(jax.random.fold_in(jax.random.fold_in(own_key, 6), position), (shards_of,), jnp.float32, smallest / len(pieces), top_value / len(pieces))
        return jnp.repeat(jnp.exp(draws), dims[position] // shards_of).reshape((-1,) + (1,) * (len(dims) - position - 1))

    level = one(*pieces[0])
    for cut in pieces[1:]:
        level = level * one(*cut)
    return level


def normal_values(stream_key, shape, deviation, bound, split=(), kind=jnp.bfloat16):
    entries = deviation * jax.random.normal(stream_key, shape, jnp.float32)
    if split:
        entries = entries * steps_of(stream_key, shape, split, -0.22, 0.18)
    return jnp.clip(entries, -bound, bound).astype(kind)


def setup_inputs(seed: int = 0) -> dict:
    streams_of = jax.random.split(jax.random.key(seed), 9)
    return {
        "zonal_wind": normal_values(streams_of[0], (NLEV, NODES, NELEM), 1.0, 6.0, ((0, 8), (2, 64)), jnp.float32),
        "meridional_wind": normal_values(streams_of[1], (NLEV, NODES, NELEM), 1.0, 6.0, ((0, 8), (2, 64)), jnp.float32),
        "vertical_wind": normal_values(streams_of[2], (NLEV, NODES, NELEM), 1.0, 6.0, ((0, 8), (2, 64)), jnp.float32),
        "pressure": normal_values(streams_of[3], (NLEV, NODES, NELEM), 1.0, 6.0, ((0, 8), (2, 64)), jnp.float32),
        "geopotential": normal_values(streams_of[4], (NLEV, NODES, NELEM), 1.0, 6.0, ((0, 8), (2, 64)), jnp.float32),
        "layer_mass": jnp.clip(jnp.exp(math.log(2.0) - 1.3862944 * jax.random.uniform(streams_of[5], (NLEV, NODES, NELEM), jnp.float32) ** steps_of(streams_of[5], (NLEV, NODES, NELEM), ((0, 8), (2, 64)), -0.2, 0.2)), 0.5, 2.0),
        "stiffness": jnp.clip(jnp.exp(math.log(1024.0) - 5.5451774 * jax.random.uniform(streams_of[6], (NLEV, NODES, NELEM), jnp.float32) ** steps_of(streams_of[6], (NLEV, NODES, NELEM), ((1, 8), (2, 64)), -0.2, 0.2)), 4.0, 1024.0),
        "elem_order": jax.vmap(lambda own: jax.random.permutation(own, EY))(jax.random.split(streams_of[7], STRIPS)).reshape((STRIPS, EY)).astype(jnp.int32),
    }


horizontal_speed = 0.12
drift_first = 0.1
drift_second = 0.06
geopotential_rate = 2.0

def gll_tables():
    points = np.array([-1.0, -1.0 / math.sqrt(5.0), 1.0 / math.sqrt(5.0), 1.0])
    quadrature = np.array([1.0 / 6.0, 5.0 / 6.0, 5.0 / 6.0, 1.0 / 6.0])
    derivative = np.zeros((4, 4))
    for target in range(4):
        for source in range(4):
            if target == source:
                derivative[target, source] = sum((1.0 / (points[target] - points[other]) for other in range(4) if other != target))
            else:
                top_term = math.prod((points[target] - points[other] for other in range(4) if other != target))
                low_term = math.prod((points[source] - points[other] for other in range(4) if other != source))
                derivative[target, source] = top_term / (low_term * (points[target] - points[source]))
    return (jnp.asarray(derivative), jnp.asarray(np.outer(quadrature, quadrature).reshape(16)))

def along_first(field, derivative):
    return jnp.einsum('ai,lijxy->lajxy', derivative, field, precision=lax.Precision.HIGHEST)

def along_second(field, derivative):
    return jnp.einsum('aj,lijxy->liaxy', derivative, field, precision=lax.Precision.HIGHEST)

def assemble(field):
    summed = field[:, 3] + jnp.roll(field[:, 0], -1, axis=2)
    field = jnp.concatenate([jnp.roll(summed, 1, axis=2)[:, None], field[:, 1:3], summed[:, None]], 1)
    summed = field[:, :, 3] + jnp.roll(field[:, :, 0], -1, axis=3)
    return jnp.concatenate([jnp.roll(summed, 1, axis=3)[:, :, None], field[:, :, 1:3], summed[:, :, None]], 2)

def reference(zonal_wind, meridional_wind, vertical_wind, pressure, geopotential, layer_mass, stiffness, elem_order):
    derivative, weights = gll_tables()
    inverse = jnp.argsort(elem_order, axis=1).astype(jnp.int32)
    strip_base = (jnp.arange(STRIPS, dtype=jnp.int32) * EY)[:, None]
    grid_index = (strip_base + inverse).reshape(-1)
    store_index = (strip_base + elem_order).reshape(-1)

    def to_grid(field):
        return jnp.take(field, grid_index, axis=2).reshape(field.shape[0], 4, 4, STRIPS, EY)

    def to_store(field):
        return jnp.take(field.reshape(NLEV, 16, NELEM), store_index, axis=2)
    mass = to_grid(layer_mass * weights[None, :, None])
    recip = 1.0 / assemble(mass)
    coeff = to_grid(stiffness)
    root = jnp.sqrt(coeff)
    coeff_last = jnp.moveaxis(coeff, 0, -1)
    zero_col = jnp.zeros_like(coeff_last[..., :1])
    lower = jnp.concatenate([zero_col, -coeff_last[..., 1:]], -1)
    upper = jnp.concatenate([-coeff_last[..., :-1], zero_col], -1)
    middle = 1.0 + 2.0 * coeff_last
    zonal = to_grid(zonal_wind)
    meridional = to_grid(meridional_wind)
    upward = to_grid(vertical_wind)
    press = to_grid(pressure)
    geopot = to_grid(geopotential)
    widths = ((1, 1), (0, 0), (0, 0), (0, 0), (0, 0))
    for step in range(SUBSTEPS):
        new_zonal = zonal + recip * assemble(mass * (-horizontal_speed * along_first(press, derivative)))
        new_merid = meridional + recip * assemble(mass * (-horizontal_speed * along_second(press, derivative)))
        new_upward = upward + recip * assemble(mass * -(drift_first * along_first(upward, derivative) + drift_second * along_second(upward, derivative)))
        new_geopot = geopot + recip * assemble(mass * -(drift_first * along_first(geopot, derivative) + drift_second * along_second(geopot, derivative)))
        zonal, meridional, upward, geopot = (new_zonal, new_merid, new_upward, new_geopot)
        divergence = along_first(zonal, derivative) + along_second(meridional, derivative)
        press = press + recip * assemble(mass * (-horizontal_speed * divergence))
        padded = jnp.pad(press, widths)
        rhs = upward - root * 0.5 * (padded[2:] - padded[:-2])
        solved = lax.linalg.tridiagonal_solve(lower, middle, upper, jnp.moveaxis(rhs, 0, -1)[..., None])[..., 0]
        solved = jnp.moveaxis(solved, -1, 0)
        padded = jnp.pad(solved, widths)
        press = press - root * 0.5 * (padded[2:] - padded[:-2])
        geopot = geopot + geopotential_rate * solved
        upward = solved
    return (to_store(zonal), to_store(meridional), to_store(upward), to_store(press), to_store(geopot))
```

```python
import functools
import math

import jax
import jax.numpy as jnp
import numpy as np
from jax import lax
from jax.experimental import pallas as pl
from jax.experimental.pallas import tpu as pltpu
from jax.sharding import PartitionSpec as P

SUBSTEPS = 3
SPEED = 0.12
DRIFT1 = 0.1
DRIFT2 = 0.06
RATE = 2.0
F32 = jnp.float32
LANES = 128
NL = 16
ROWS = 36
PAD = 40


def tables():
    points = np.array([-1.0, -1.0 / math.sqrt(5.0), 1.0 / math.sqrt(5.0), 1.0])
    quad = [1.0 / 6.0, 5.0 / 6.0, 5.0 / 6.0, 1.0 / 6.0]
    d = np.zeros((4, 4))
    for t in range(4):
        for s in range(4):
            if t == s:
                d[t, s] = sum(1.0 / (points[t] - points[o]) for o in range(4) if o != t)
            else:
                top = math.prod(points[t] - points[o] for o in range(4) if o != t)
                low = math.prod(points[s] - points[o] for o in range(4) if o != s)
                d[t, s] = top / (low * (points[t] - points[s]))
    d[np.abs(d) < 1e-12] = 0.0
    return [[float(x) for x in row] for row in d], [float(a * b) for a in quad for b in quad]


D, WEIGHT = tables()


def lin(coeffs, values):
    total = None
    for c, v in zip(coeffs, values):
        if c != 0.0:
            total = c * v if total is None else total + c * v
    return total


def up(x):
    return pltpu.roll(x, LANES - 1, 1)


def down(x):
    return pltpu.roll(x, 1, 1)


def sew(row):
    last = row[3] + up(row[0])
    return [down(last), row[1], row[2], last]


def rows(ref, n):
    return ref[n * NL : (n + 1) * NL, :]


def put(ref, n, value):
    ref[n * NL : (n + 1) * NL, :] = value


def dx(get, i, j):
    return lin(D[i], [get(k * 4 + j) for k in range(4)])


def dy(get, i, j):
    return lin(D[j], [get(i * 4 + k) for k in range(4)])


def three(ref, base):
    a, b, c = (rows(ref, base + k) for k in range(3))
    return [down(c), a, b, c]


def place():
    core = lax.rem(lax.axis_index("elem"), 2)
    return core, (1 - 2 * core).astype(F32)


def inverse_of(order_ref):
    order = order_ref[...].astype(F32)
    across = jnp.broadcast_to(order, (LANES, LANES))
    along = across.T
    lane = lax.broadcasted_iota(jnp.int32, (LANES, LANES), 1).astype(F32)
    slot = lax.broadcasted_iota(jnp.int32, (LANES, LANES), 0).astype(F32)
    return jnp.sum(jnp.where(along == lane, slot, 0.0), axis=0, keepdims=True).astype(jnp.int32)


def pick(values, index):
    return jnp.take_along_axis(values, index, axis=1, mode="promise_in_bounds")


def stage_a(sg, src, p, m, r, dst, ta, tb):
    for f in range(4):
        if f < 2:
            get = functools.partial(rows, p)
        else:
            get = functools.partial(rows, src[f])
        for i in range(4):
            row = []
            for j in range(4):
                if f == 0:
                    t = (-SPEED * sg) * dx(get, i, j)
                elif f == 1:
                    t = -SPEED * dy(get, i, j)
                else:
                    t = -((DRIFT1 * sg) * dx(get, i, j) + DRIFT2 * dy(get, i, j))
                row.append(rows(m, i * 4 + j) * t)
            row = sew(row)
            for j in range(4):
                n = i * 4 + j
                own = rows(src[f], n)
                if i in (1, 2):
                    put(dst[f], n, own + rows(r, n) * row[j])
                else:
                    put(dst[f], n, own)
                    if j > 0:
                        put(ta if i == 3 else tb, f * 3 + j - 1, row[j])


def k_init(order, u_in, v_in, w_in, p_in, g_in, lm_in, u, v, w, g, p, m, r, ta, tb, us, vs, ws, gs):
    core, sg = place()
    index = jnp.broadcast_to(inverse_of(order), (NL, LANES))
    for src, dst in ((p_in, p), (lm_in, m), (u_in, us), (v_in, vs), (w_in, ws), (g_in, gs)):
        for i in range(4):
            for j in range(4):
                start = jnp.where(core == 1, (3 - i) * 4 + j, i * 4 + j)
                value = pick(src[pl.ds(start, NL, stride=16), :], index)
                if dst is m:
                    value = value * WEIGHT[i * 4 + j]
                put(dst, i * 4 + j, value)
    for i in range(4):
        row = sew([rows(m, i * 4 + j) for j in range(4)])
        for j in range(4):
            if i in (1, 2):
                put(r, i * 4 + j, 1.0 / row[j])
            else:
                put(r, i * 4 + j, row[j])
                if j > 0:
                    put(ta if i == 3 else tb, 12 + j - 1, row[j])
    stage_a(sg, (us, vs, ws, gs), p, m, r, (u, v, w, g), ta, tb)


def k_b(first, *refs):
    if first:
        u, v, w, g, m, r, ta, ra, tb, f3, bm, r3 = refs
        own, got = three(ta, 12), three(ra, 12)
        for j in range(4):
            put(r3, j, 1.0 / (own[j] + got[j]))
        rr = lambda j: rows(r3, j)
    else:
        u, v, w, g, r, ta, ra, tb, f3, bm = refs
        rr = lambda j: rows(r, 12 + j)
    _, sg = place()
    for f, field in enumerate((u, v, w, g)):
        own, got = three(ta, f * 3), three(ra, f * 3)
        for j in range(4):
            put(f3, f * 4 + j, rows(field, 12 + j) + rr(j) * (own[j] + got[j]))
    for j in range(4):
        along = lin(D[0], [rows(u, j), rows(u, 4 + j), rows(u, 8 + j), rows(f3, j)])
        across = dy(functools.partial(rows, v), 0, j)
        put(bm, 12 + j, sg * along + across)
    for k in range(12):
        put(bm, k, rows(tb, k))
    if first:
        for j in range(4):
            put(bm, 16 + j, rows(m, j))


def k_c(first, *refs):
    if first:
        u, v, w, g, p, m, r, r3, f3, tb, rb, uo, vo, wo, go, po, dm, ro, mo = refs
        own, got = three(tb, 12), sew([rows(rb, 16 + j) for j in range(4)])
        for j in range(4):
            put(ro, j, 1.0 / (own[j] + got[j]))
            put(ro, 12 + j, rows(r3, j))
            put(mo, j, rows(rb, 16 + j))
            for i in (1, 2):
                put(ro, i * 4 + j, rows(r, i * 4 + j))
        r, mn = ro, mo
    else:
        u, v, w, g, p, m, r, mn, f3, tb, rb, uo, vo, wo, go, po, dm = refs
    _, sg = place()
    inc = []
    for f, (field, out) in enumerate(((u, uo), (v, vo), (w, wo), (g, go))):
        own, got = three(tb, f * 3), three(rb, f * 3)
        part = []
        for j in range(4):
            add = rows(r, j) * (own[j] + got[j])
            part.append(add)
            put(out, j, rows(field, j) + add)
            put(out, 12 + j, rows(f3, f * 4 + j))
            for i in (1, 2):
                put(out, i * 4 + j, rows(field, i * 4 + j))
        if f < 2:
            inc.append(part)
    other = []
    for j in range(4):
        t = rows(rb, 12 + j) - (sg * D[0][0]) * inc[0][j] + lin(D[j], inc[1])
        other.append(rows(mn, j) * (-SPEED * t))
    other = sew(other)
    gu, gv = functools.partial(rows, uo), functools.partial(rows, vo)
    for i in range(4):
        row = sew([rows(m, i * 4 + j) * (-SPEED * (sg * dx(gu, i, j) + dy(gv, i, j))) for j in range(4)])
        for j in range(4):
            n = i * 4 + j
            total = row[j] + other[j] if i == 0 else row[j]
            put(po, n, rows(p, n) + rows(r, n) * total)
            if i == 3 and j > 0:
                put(dm, j - 1, row[j])


def level(ref, k):
    return jnp.concatenate([ref[pl.ds(k, 8, stride=32), :], ref[pl.ds(16 + k, 8, stride=32), :]], 0)


def node_of(ref, n):
    return ref[pl.ds((n % 2) * 8 + n // 2, NL, stride=16), :]


def k_d(p, w, r, rd, wu, pu, wd, pd, po, vm):
    me = lax.axis_index("lev")
    got = three(rd, 0)
    for n in range(12):
        put(po, n, rows(p, n))
    for j in range(4):
        put(po, 12 + j, rows(p, 12 + j) + rows(r, 12 + j) * got[j])
    su = sd = None
    for k in range(NL):
        wk, pk = level(w, k), level(po, k)
        a = rows(wu, k) * wk + rows(pu, k) * pk
        b = rows(wd, k) * wk + rows(pd, k) * pk
        su = a if su is None else su + a
        sd = b if sd is None else sd + b
    low, high = level(po, 0), level(po, NL - 1)
    for c in range(8):
        above = c > me
        vm[c * 32 : c * 32 + 16, :] = jnp.where(above, su, sd)
        vm[c * 32 + 16 : c * 32 + 32, :] = jnp.where(above, high, low)


def solve(p, w, rv, ia, hr, rh, cp, cc, edge, s_out, p_out):
    me = lax.axis_index("lev")
    low, high = level(p, 0), level(p, NL - 1)
    from_below = -rows(edge, 0) * low
    from_above = rows(edge, 1) * high
    for c in range(8):
        part = rows(cc, 2 * c) * rows(rv, 2 * c) + rows(cc, 2 * c + 1) * rows(rv, 2 * c + 1)
        from_below = from_below + jnp.where(c < me, part, 0.0)
        from_above = from_above + jnp.where(c > me, part, 0.0)
    prev = rv[pl.ds(pl.multiple_of(jnp.maximum(me - 1, 0) * 32 + 16, 16), 16), :]
    then = rv[pl.ds(pl.multiple_of(jnp.minimum(me + 1, 7) * 32 + 16, 16), 16), :]
    prev = jnp.where(me > 0, prev, 0.0)
    then = jnp.where(me < 7, then, 0.0)
    d = []
    last = from_below
    for k in range(NL):
        below = level(p, k - 1) if k > 0 else prev
        above = level(p, k + 1) if k < NL - 1 else then
        q = level(w, k) * rows(ia, k) - (above - below) * rows(hr, k)
        last = rows(cp, k) * (q + last)
        d.append(last)
    s = (d[NL - 1] + rows(cp, NL - 1) * from_above) * rows(edge, 2)
    after = from_above + rows(edge, 4) * s
    for k in range(NL - 1, -1, -1):
        put(s_out, k, s)
        if k > 0:
            nxt = d[k - 1] + rows(cp, k - 1) * s
        else:
            nxt = from_below + rows(edge, 3) * s
        put(p_out, k, level(p, k) - rows(rh, k) * (after - nxt))
        after, s = s, nxt


def k_e(p, w, g, u, v, rv, ia, hr, rh, cp, cc, edge, m, r, uo, vo, wo, go, po, ta, tb, ss, ps, ws, gs):
    _, sg = place()
    solve(p, w, rv, ia, hr, rh, cp, cc, edge, ss, ps)
    for n in range(16):
        s = node_of(ss, n)
        put(ws, n, s)
        put(gs, n, rows(g, n) + RATE * s)
        put(po, n, node_of(ps, n))
    stage_a(sg, (u, v, ws, gs), po, m, r, (uo, vo, wo, go), ta, tb)


def k_out(order, p, w, g, u, v, rv, ia, hr, rh, cp, cc, edge, uo, vo, wo, po, go, ss, ps):
    core, _ = place()
    solve(p, w, rv, ia, hr, rh, cp, cc, edge, ss, ps)
    index = jnp.broadcast_to(order[...], (NL, LANES))
    for i in range(4):
        for j in range(4):
            n = i * 4 + j
            start = jnp.where(core == 1, (3 - i) * 4 + j, n)
            s = node_of(ss, n)
            for out, value in (
                (uo, rows(u, n)),
                (vo, rows(v, n)),
                (wo, s),
                (po, node_of(ps, n)),
                (go, rows(g, n) + RATE * s),
            ):
                out[pl.ds(start, NL, stride=16), :] = pick(value, index)


def k_col(order, st, out, a_s, ia_s):
    index = jnp.broadcast_to(inverse_of(order), (NL, LANES))
    for k in range(16):
        a = pick(st[k * 16 : k * 16 + 16, :], index)
        a_s[k * 16 : k * 16 + 16, :] = a
        ia_s[k * 16 : k * 16 + 16, :] = 1.0 / a
    one = jnp.ones((2, LANES), F32)
    zero = jnp.zeros((2, LANES), F32)
    pair = lambda ref, k: ref[2 * k : 2 * k + 2, :]
    th, de = one, one
    th_last, rho = [], [one]
    for k in range(128):
        de = de + th * pair(ia_s, k)
        th = th + de
        if k % 16 == 15:
            th_last.append(th)
            rho.append(de / th)
    ps, de = one, one
    ps_first, sig = [None] * 8, [None] * 9
    sig[8] = one
    for k in range(127, -1, -1):
        de = de + ps * pair(ia_s, k)
        ps = ps + de
        if k % 16 == 0:
            ps_first[k // 16] = ps
            sig[k // 16] = de / ps
    inv_th = [1.0 / x for x in th_last]
    inv_ps = [1.0 / x for x in ps_first]
    half = lambda k: 0.5 * jnp.sqrt(pair(ia_s, k))
    lo_half = [half(16 * c + 16) if c < 7 else zero for c in range(8)]
    hi_half = [half(16 * c - 1) if c > 0 else zero for c in range(8)]
    for b in range(8):
        def send(t, value):
            out[b * 80 + 2 * t : b * 80 + 2 * t + 2, :] = value

        for k in range(16):
            send(k, pair(a_s, b * 16 + k))
        for c in range(8):
            cs = cq = zero
            if c < b:
                cs = th_last[c] * inv_th[b - 1]
                if c < b - 1:
                    cq = cs * lo_half[c]
            elif c > b:
                cs = ps_first[c] * inv_ps[b + 1]
                if c > b + 1:
                    cq = -cs * hi_half[c]
            send(16 + 2 * c, cs)
            send(17 + 2 * c, cq)
        send(32, rho[b])
        send(33, sig[b + 1])
        send(34, hi_half[b])
        send(35, lo_half[b])
        for t in range(ROWS, PAD):
            send(t, zero)


def k_stat(got, ia, hr, rh, cp, wu, pu, wd, pd, cc, edge, scr, tu_s, td_s):
    core, _ = place()
    for s in range(8):
        src = jnp.where(core == 1, s ^ 6, s)
        scr[s * 80 : (s + 1) * 80, :] = got[pl.ds(pl.multiple_of(src * 80, 8), 80), :]

    def row(t):
        return jnp.concatenate([scr[pl.ds(2 * t + e, 8, stride=80), :] for e in range(2)], 0)

    for k in range(NL):
        a = row(k)
        ra = 1.0 / a
        root = jnp.sqrt(a)
        put(ia, k, ra)
        put(rh, k, 0.5 * root)
        put(hr, k, 0.5 * (ra * root))
    for t in range(16):
        put(cc, t, row(16 + t))
    rho, sig, h_lo, h_hi = row(32), row(33), row(34), row(35)
    th, de = jnp.ones_like(rho), rho
    for k in range(NL):
        de = de + th * rows(ia, k)
        new = th + de
        put(cp, k, th / new)
        put(tu_s, k, th)
        th = new
    inv_th = 1.0 / th
    ps, de = jnp.ones_like(rho), sig
    for k in range(NL - 1, -1, -1):
        de = de + ps * rows(ia, k)
        put(td_s, k, ps)
        ps = ps + de
    inv_ps = 1.0 / ps
    for ref, inv in ((tu_s, inv_th), (td_s, inv_ps)):
        for k in range(NL):
            put(ref, k, rows(ref, k) * inv)
    cpm, cqp = 1.0 - rho, 1.0 - sig
    for ref, wt, pt, in ((tu_s, wu, pu), (td_s, wd, pd)):
        for k in range(NL):
            put(wt, k, rows(ref, k) * rows(ia, k))
            value = None
            if k < NL - 1:
                value = rows(ref, k + 1) * rows(hr, k + 1)
            elif ref is td_s:
                value = rows(ref, k) * cqp * h_hi
            else:
                value = jnp.zeros_like(rho)
            if k > 0:
                value = value - rows(ref, k - 1) * rows(hr, k - 1)
            elif ref is tu_s:
                value = value - rows(ref, 0) * cpm * h_lo
            put(pt, k, value)
    put(edge, 0, cpm * h_lo)
    put(edge, 1, cqp * h_hi)
    put(edge, 2, 1.0 / (1.0 - rows(cp, NL - 1) * cqp))
    put(edge, 3, cpm)
    put(edge, 4, cqp)


def call(kernel, name, args, outs, scratch=()):
    vmem = pl.BlockSpec(memory_space=pltpu.VMEM)
    return pl.pallas_call(
        kernel,
        out_shape=[jax.ShapeDtypeStruct((n * NL, LANES), F32) for n in outs],
        in_specs=[vmem] * len(args),
        out_specs=[vmem] * len(outs),
        scratch_shapes=[pltpu.VMEM((n * NL, LANES), F32) for n in scratch],
        name=name,
    )(*args)


def body(zonal, meridional, vertical, pressure, geopotential, layer_mass, stiffness, order):
    count = lax.axis_size("elem")
    mates = [(i, i ^ 1) for i in range(count)]
    others = [(i, (i + 1) % count if i % 2 else (i - 1) % count) for i in range(count)]
    flat = lambda x: x.reshape(-1, LANES)
    u, v, w, p, g, lm = (flat(x) for x in (zonal, meridional, vertical, pressure, geopotential, layer_mass))

    def swap_levels(x):
        return lax.all_to_all(x.reshape(8, -1, LANES), "lev", 0, 0, tiled=True).reshape(-1, LANES)

    (sent,) = call(k_col, "col", [order, flat(stiffness)], [40], [16, 16])
    got = swap_levels(sent)
    u, v, w, g, p, m, r, ta, tb = call(
        k_init, "init", [order, u, v, w, p, g, lm], [16] * 7 + [15, 15], [16] * 4
    )
    mn = r3 = None
    statics = None
    for step in range(SUBSTEPS):
        first = step == 0
        ra = lax.ppermute(ta, "elem", mates)
        if first:
            f3, bm, r3 = call(functools.partial(k_b, True), "b1", [u, v, w, g, m, r, ta, ra, tb], [16, 20, 4])
        else:
            f3, bm = call(functools.partial(k_b, False), "b", [u, v, w, g, r, ta, ra, tb], [16, 16])
        rb = lax.ppermute(bm, "elem", others)
        if first:
            u, v, w, g, p, dm, r, mn = call(
                functools.partial(k_c, True),
                "c1",
                [u, v, w, g, p, m, r, r3, f3, tb, rb],
                [16] * 5 + [3, 16, 4],
            )
        else:
            u, v, w, g, p, dm = call(
                functools.partial(k_c, False), "c", [u, v, w, g, p, m, r, mn, f3, tb, rb], [16] * 5 + [3]
            )
        rd = lax.ppermute(dm, "elem", mates)
        if first:
            ia, hr, rh, cp, wu, pu, wd, pd, cc, edge = call(
                k_stat, "stat", [got], [16] * 8 + [16, 5], [40, 16, 16]
            )
            statics = [ia, hr, rh, cp, cc, edge]
        p, vm = call(k_d, "d", [p, w, r, rd, wu, pu, wd, pd], [16, 16])
        rv = swap_levels(vm)
        if step < SUBSTEPS - 1:
            u, v, w, g, p, ta, tb = call(
                k_e, "e", [p, w, g, u, v, rv] + statics + [m, r], [16] * 5 + [12, 12], [16] * 4
            )
        else:
            outs = call(k_out, "out", [order, p, w, g, u, v, rv] + statics, [16] * 5, [16] * 2)
    return tuple(x.reshape(zonal.shape) for x in outs)


def solution(mesh):
    fields = P("lev", None, "elem")
    return jax.shard_map(
        body,
        mesh=mesh,
        in_specs=(fields,) * 6 + (P(None, "lev", "elem"), P("elem", None)),
        out_specs=(fields,) * 5,
        check_vma=False,
    )
```

```python
import functools
import math

import jax
import jax.numpy as jnp
import numpy as np
from jax import lax
from jax.experimental import pallas as pl
from jax.experimental.pallas import tpu as pltpu
from jax.sharding import PartitionSpec as P

SUBSTEPS = 3
SPEED = 0.12
DRIFT1 = 0.1
DRIFT2 = 0.06
RATE = 2.0
F32 = jnp.float32
LANES = 128
NL = 16
ROWS = 36
PAD = 40


def tables():
    points = np.array([-1.0, -1.0 / math.sqrt(5.0), 1.0 / math.sqrt(5.0), 1.0])
    quad = [1.0 / 6.0, 5.0 / 6.0, 5.0 / 6.0, 1.0 / 6.0]
    d = np.zeros((4, 4))
    for t in range(4):
        for s in range(4):
            if t == s:
                d[t, s] = sum(1.0 / (points[t] - points[o]) for o in range(4) if o != t)
            else:
                top = math.prod(points[t] - points[o] for o in range(4) if o != t)
                low = math.prod(points[s] - points[o] for o in range(4) if o != s)
                d[t, s] = top / (low * (points[t] - points[s]))
    d[np.abs(d) < 1e-12] = 0.0
    return [[float(x) for x in row] for row in d], [float(a * b) for a in quad for b in quad]


D, WEIGHT = tables()


def lin(coeffs, values):
    total = None
    for c, v in zip(coeffs, values):
        if c != 0.0:
            total = c * v if total is None else total + c * v
    return total


def up(x):
    return pltpu.roll(x, LANES - 1, 1)


def down(x):
    return pltpu.roll(x, 1, 1)


def sew(row):
    last = row[3] + up(row[0])
    return [down(last), row[1], row[2], last]


def rows(ref, n):
    return ref[n * NL : (n + 1) * NL, :]


def put(ref, n, value):
    ref[n * NL : (n + 1) * NL, :] = value


def dx(get, i, j):
    return lin(D[i], [get(k * 4 + j) for k in range(4)])


def dy(get, i, j):
    return lin(D[j], [get(i * 4 + k) for k in range(4)])


def three(ref, base):
    a, b, c = (rows(ref, base + k) for k in range(3))
    return [down(c), a, b, c]


def place():
    core = lax.rem(lax.axis_index("elem"), 2)
    return core, (1 - 2 * core).astype(F32)


def inverse_of(order_ref):
    order = order_ref[...].astype(F32)
    across = jnp.broadcast_to(order, (LANES, LANES))
    along = across.T
    lane = lax.broadcasted_iota(jnp.int32, (LANES, LANES), 1).astype(F32)
    slot = lax.broadcasted_iota(jnp.int32, (LANES, LANES), 0).astype(F32)
    return jnp.sum(jnp.where(along == lane, slot, 0.0), axis=0, keepdims=True).astype(jnp.int32)


def pick(values, index):
    return jnp.take_along_axis(values, index, axis=1, mode="promise_in_bounds")


def stage_a(sg, src, p, m, r, dst, ta, tb):
    for f in range(4):
        if f < 2:
            get = functools.partial(rows, p)
        else:
            get = functools.partial(rows, src[f])
        for i in range(4):
            row = []
            for j in range(4):
                if f == 0:
                    t = (-SPEED * sg) * dx(get, i, j)
                elif f == 1:
                    t = -SPEED * dy(get, i, j)
                else:
                    t = -((DRIFT1 * sg) * dx(get, i, j) + DRIFT2 * dy(get, i, j))
                row.append(rows(m, i * 4 + j) * t)
            row = sew(row)
            for j in range(4):
                n = i * 4 + j
                own = rows(src[f], n)
                if i in (1, 2):
                    put(dst[f], n, own + rows(r, n) * row[j])
                else:
                    put(dst[f], n, own)
                    if j > 0:
                        put(ta if i == 3 else tb, f * 3 + j - 1, row[j])


def k_init(order, u_in, v_in, w_in, p_in, g_in, lm_in, u, v, w, g, p, m, r, ta, tb, us, vs, ws, gs):
    core, sg = place()
    index = jnp.broadcast_to(inverse_of(order), (NL, LANES))
    for src, dst in ((p_in, p), (lm_in, m), (u_in, us), (v_in, vs), (w_in, ws), (g_in, gs)):
        for i in range(4):
            for j in range(4):
                start = jnp.where(core == 1, (3 - i) * 4 + j, i * 4 + j)
                value = pick(src[pl.ds(start, NL, stride=16), :], index)
                if dst is m:
                    value = value * WEIGHT[i * 4 + j]
                put(dst, i * 4 + j, value)
    for i in range(4):
        row = sew([rows(m, i * 4 + j) for j in range(4)])
        for j in range(4):
            if i in (1, 2):
                put(r, i * 4 + j, 1.0 / row[j])
            else:
                put(r, i * 4 + j, row[j])
                if j > 0:
                    put(ta if i == 3 else tb, 12 + j - 1, row[j])
    stage_a(sg, (us, vs, ws, gs), p, m, r, (u, v, w, g), ta, tb)


def k_b(first, *refs):
    if first:
        u, v, w, g, m, r, ta, ra, tb, f3, bm, r3 = refs
        own, got = three(ta, 12), three(ra, 12)
        for j in range(4):
            put(r3, j, 1.0 / (own[j] + got[j]))
        rr = lambda j: rows(r3, j)
    else:
        u, v, w, g, r, ta, ra, tb, f3, bm = refs
        rr = lambda j: rows(r, 12 + j)
    _, sg = place()
    for f, field in enumerate((u, v, w, g)):
        own, got = three(ta, f * 3), three(ra, f * 3)
        for j in range(4):
            put(f3, f * 4 + j, rows(field, 12 + j) + rr(j) * (own[j] + got[j]))
    for j in range(4):
        along = lin(D[0], [rows(u, j), rows(u, 4 + j), rows(u, 8 + j), rows(f3, j)])
        across = dy(functools.partial(rows, v), 0, j)
        put(bm, 12 + j, sg * along + across)
    for k in range(12):
        put(bm, k, rows(tb, k))
    if first:
        for j in range(4):
            put(bm, 16 + j, rows(m, j))


def k_c(first, *refs):
    if first:
        u, v, w, g, p, m, r, r3, f3, tb, rb, uo, vo, wo, go, po, dm, ro, mo = refs
        own, got = three(tb, 12), sew([rows(rb, 16 + j) for j in range(4)])
        for j in range(4):
            put(ro, j, 1.0 / (own[j] + got[j]))
            put(ro, 12 + j, rows(r3, j))
            put(mo, j, rows(rb, 16 + j))
            for i in (1, 2):
                put(ro, i * 4 + j, rows(r, i * 4 + j))
        r, mn = ro, mo
    else:
        u, v, w, g, p, m, r, mn, f3, tb, rb, uo, vo, wo, go, po, dm = refs
    _, sg = place()
    inc = []
    for f, (field, out) in enumerate(((u, uo), (v, vo), (w, wo), (g, go))):
        own, got = three(tb, f * 3), three(rb, f * 3)
        part = []
        for j in range(4):
            add = rows(r, j) * (own[j] + got[j])
            part.append(add)
            put(out, j, rows(field, j) + add)
            put(out, 12 + j, rows(f3, f * 4 + j))
            for i in (1, 2):
                put(out, i * 4 + j, rows(field, i * 4 + j))
        if f < 2:
            inc.append(part)
    other = []
    for j in range(4):
        t = rows(rb, 12 + j) - (sg * D[0][0]) * inc[0][j] + lin(D[j], inc[1])
        other.append(rows(mn, j) * (-SPEED * t))
    other = sew(other)
    gu, gv = functools.partial(rows, uo), functools.partial(rows, vo)
    for i in range(4):
        row = sew([rows(m, i * 4 + j) * (-SPEED * (sg * dx(gu, i, j) + dy(gv, i, j))) for j in range(4)])
        for j in range(4):
            n = i * 4 + j
            total = row[j] + other[j] if i == 0 else row[j]
            put(po, n, rows(p, n) + rows(r, n) * total)
            if i == 3 and j > 0:
                put(dm, j - 1, row[j])


def level(ref, k):
    return jnp.concatenate([ref[pl.ds(k, 8, stride=32), :], ref[pl.ds(16 + k, 8, stride=32), :]], 0)


def node_of(ref, n):
    return ref[pl.ds((n % 2) * 8 + n // 2, NL, stride=16), :]


def k_d(p, w, r, rd, wu, pu, wd, pd, po, vm):
    me = lax.axis_index("lev")
    got = three(rd, 0)
    for n in range(12):
        put(po, n, rows(p, n))
    for j in range(4):
        put(po, 12 + j, rows(p, 12 + j) + rows(r, 12 + j) * got[j])
    su = sd = None
    for k in range(NL):
        wk, pk = level(w, k), level(po, k)
        a = rows(wu, k) * wk + rows(pu, k) * pk
        b = rows(wd, k) * wk + rows(pd, k) * pk
        su = a if su is None else su + a
        sd = b if sd is None else sd + b
    low, high = level(po, 0), level(po, NL - 1)
    for c in range(8):
        above = c > me
        vm[c * 32 : c * 32 + 16, :] = jnp.where(above, su, sd)
        vm[c * 32 + 16 : c * 32 + 32, :] = jnp.where(above, high, low)


def solve(p, w, rv, ia, hr, rh, cp, cc, edge, s_out, p_out):
    me = lax.axis_index("lev")
    low, high = level(p, 0), level(p, NL - 1)
    from_below = -rows(edge, 0) * low
    from_above = rows(edge, 1) * high
    for c in range(8):
        part = rows(cc, 2 * c) * rows(rv, 2 * c) + rows(cc, 2 * c + 1) * rows(rv, 2 * c + 1)
        from_below = from_below + jnp.where(c < me, part, 0.0)
        from_above = from_above + jnp.where(c > me, part, 0.0)
    prev = rv[pl.ds(pl.multiple_of(jnp.maximum(me - 1, 0) * 32 + 16, 16), 16), :]
    then = rv[pl.ds(pl.multiple_of(jnp.minimum(me + 1, 7) * 32 + 16, 16), 16), :]
    prev = jnp.where(me > 0, prev, 0.0)
    then = jnp.where(me < 7, then, 0.0)
    d = []
    last = from_below
    for k in range(NL):
        below = level(p, k - 1) if k > 0 else prev
        above = level(p, k + 1) if k < NL - 1 else then
        q = level(w, k) * rows(ia, k) - (above - below) * rows(hr, k)
        last = rows(cp, k) * (q + last)
        d.append(last)
    s = (d[NL - 1] + rows(cp, NL - 1) * from_above) * rows(edge, 2)
    after = from_above + rows(edge, 4) * s
    for k in range(NL - 1, -1, -1):
        put(s_out, k, s)
        if k > 0:
            nxt = d[k - 1] + rows(cp, k - 1) * s
        else:
            nxt = from_below + rows(edge, 3) * s
        put(p_out, k, level(p, k) - rows(rh, k) * (after - nxt))
        after, s = s, nxt


def k_e(p, w, g, u, v, rv, ia, hr, rh, cp, cc, edge, m, r, uo, vo, wo, go, po, ta, tb, ss, ps, ws, gs):
    _, sg = place()
    solve(p, w, rv, ia, hr, rh, cp, cc, edge, ss, ps)
    for n in range(16):
        s = node_of(ss, n)
        put(ws, n, s)
        put(gs, n, rows(g, n) + RATE * s)
        put(po, n, node_of(ps, n))
    stage_a(sg, (u, v, ws, gs), po, m, r, (uo, vo, wo, go), ta, tb)


def k_out(order, p, w, g, u, v, rv, ia, hr, rh, cp, cc, edge, uo, vo, wo, po, go, ss, ps):
    core, _ = place()
    solve(p, w, rv, ia, hr, rh, cp, cc, edge, ss, ps)
    index = jnp.broadcast_to(order[...], (NL, LANES))
    for i in range(4):
        for j in range(4):
            n = i * 4 + j
            start = jnp.where(core == 1, (3 - i) * 4 + j, n)
            s = node_of(ss, n)
            for out, value in (
                (uo, rows(u, n)),
                (vo, rows(v, n)),
                (wo, s),
                (po, node_of(ps, n)),
                (go, rows(g, n) + RATE * s),
            ):
                out[pl.ds(start, NL, stride=16), :] = pick(value, index)


def k_col(order, st, out, a_s, ia_s):
    index = jnp.broadcast_to(inverse_of(order), (NL, LANES))
    for k in range(16):
        a = pick(st[k * 16 : k * 16 + 16, :], index)
        a_s[k * 16 : k * 16 + 16, :] = a
        ia_s[k * 16 : k * 16 + 16, :] = 1.0 / a
    one = jnp.ones((2, LANES), F32)
    zero = jnp.zeros((2, LANES), F32)
    pair = lambda ref, k: ref[2 * k : 2 * k + 2, :]
    th, de = one, one
    th_last, rho = [], [one]
    for k in range(128):
        de = de + th * pair(ia_s, k)
        th = th + de
        if k % 16 == 15:
            th_last.append(th)
            rho.append(de / th)
    ps, de = one, one
    ps_first, sig = [None] * 8, [None] * 9
    sig[8] = one
    for k in range(127, -1, -1):
        de = de + ps * pair(ia_s, k)
        ps = ps + de
        if k % 16 == 0:
            ps_first[k // 16] = ps
            sig[k // 16] = de / ps
    inv_th = [1.0 / x for x in th_last]
    inv_ps = [1.0 / x for x in ps_first]
    half = lambda k: 0.5 * jnp.sqrt(pair(ia_s, k))
    lo_half = [half(16 * c + 16) if c < 7 else zero for c in range(8)]
    hi_half = [half(16 * c - 1) if c > 0 else zero for c in range(8)]
    for b in range(8):
        def send(t, value):
            out[b * 80 + 2 * t : b * 80 + 2 * t + 2, :] = value

        for k in range(16):
            send(k, pair(a_s, b * 16 + k))
        for c in range(8):
            cs = cq = zero
            if c < b:
                cs = th_last[c] * inv_th[b - 1]
                if c < b - 1:
                    cq = cs * lo_half[c]
            elif c > b:
                cs = ps_first[c] * inv_ps[b + 1]
                if c > b + 1:
                    cq = -cs * hi_half[c]
            send(16 + 2 * c, cs)
            send(17 + 2 * c, cq)
        send(32, rho[b])
        send(33, sig[b + 1])
        send(34, hi_half[b])
        send(35, lo_half[b])
        for t in range(ROWS, PAD):
            send(t, zero)


def k_stat(got, ia, hr, rh, cp, wu, pu, wd, pd, cc, edge, scr, tu_s, td_s):
    core, _ = place()
    for s in range(8):
        src = jnp.where(core == 1, s ^ 6, s)
        scr[s * 80 : (s + 1) * 80, :] = got[pl.ds(pl.multiple_of(src * 80, 8), 80), :]

    def row(t):
        return jnp.concatenate([scr[pl.ds(2 * t + e, 8, stride=80), :] for e in range(2)], 0)

    for k in range(NL):
        a = row(k)
        ra = 1.0 / a
        root = jnp.sqrt(a)
        put(ia, k, ra)
        put(rh, k, 0.5 * root)
        put(hr, k, 0.5 * (ra * root))
    for t in range(16):
        put(cc, t, row(16 + t))
    rho, sig, h_lo, h_hi = row(32), row(33), row(34), row(35)
    th, de = jnp.ones_like(rho), rho
    for k in range(NL):
        de = de + th * rows(ia, k)
        new = th + de
        put(cp, k, th / new)
        put(tu_s, k, th)
        th = new
    inv_th = 1.0 / th
    ps, de = jnp.ones_like(rho), sig
    for k in range(NL - 1, -1, -1):
        de = de + ps * rows(ia, k)
        put(td_s, k, ps)
        ps = ps + de
    inv_ps = 1.0 / ps
    for ref, inv in ((tu_s, inv_th), (td_s, inv_ps)):
        for k in range(NL):
            put(ref, k, rows(ref, k) * inv)
    cpm, cqp = 1.0 - rho, 1.0 - sig
    for ref, wt, pt, in ((tu_s, wu, pu), (td_s, wd, pd)):
        for k in range(NL):
            put(wt, k, rows(ref, k) * rows(ia, k))
            value = None
            if k < NL - 1:
                value = rows(ref, k + 1) * rows(hr, k + 1)
            elif ref is td_s:
                value = rows(ref, k) * cqp * h_hi
            else:
                value = jnp.zeros_like(rho)
            if k > 0:
                value = value - rows(ref, k - 1) * rows(hr, k - 1)
            elif ref is tu_s:
                value = value - rows(ref, 0) * cpm * h_lo
            put(pt, k, value)
    put(edge, 0, cpm * h_lo)
    put(edge, 1, cqp * h_hi)
    put(edge, 2, 1.0 / (1.0 - rows(cp, NL - 1) * cqp))
    put(edge, 3, cpm)
    put(edge, 4, cqp)


def call(kernel, name, args, outs, scratch=(), free_in=False, free_out=False):
    vmem = pl.BlockSpec(memory_space=pltpu.VMEM)
    if not free_in:
        args = [pltpu.with_memory_space_constraint(x, pltpu.VMEM) if x.dtype == F32 else x for x in args]
    kind = jax.ShapeDtypeStruct if free_out else pltpu.VMEM
    return pl.pallas_call(
        kernel,
        out_shape=[kind((n * NL, LANES), F32) for n in outs],
        in_specs=[vmem] * len(args),
        out_specs=[vmem] * len(outs),
        scratch_shapes=[pltpu.VMEM((n * NL, LANES), F32) for n in scratch],
        compiler_params=pltpu.CompilerParams(vmem_limit_bytes=8 << 20),
        name=name,
    )(*args)


def body(zonal, meridional, vertical, pressure, geopotential, layer_mass, stiffness, order):
    count = lax.axis_size("elem")
    mates = [(i, i ^ 1) for i in range(count)]
    others = [(i, (i + 1) % count if i % 2 else (i - 1) % count) for i in range(count)]
    flat = lambda x: x.reshape(-1, LANES)
    u, v, w, p, g, lm = (flat(x) for x in (zonal, meridional, vertical, pressure, geopotential, layer_mass))

    def swap_levels(x):
        return lax.all_to_all(x.reshape(8, -1, LANES), "lev", 0, 0, tiled=True).reshape(-1, LANES)

    (sent,) = call(k_col, "col", [order, flat(stiffness)], [40], [16, 16], free_in=True)
    got = swap_levels(sent)
    u, v, w, g, p, m, r, ta, tb = call(
        k_init, "init", [order, u, v, w, p, g, lm], [16] * 7 + [15, 15], [16] * 4, free_in=True
    )
    mn = r3 = None
    statics = None
    for step in range(SUBSTEPS):
        first = step == 0
        ra = lax.ppermute(ta, "elem", mates)
        if first:
            f3, bm, r3 = call(functools.partial(k_b, True), "b1", [u, v, w, g, m, r, ta, ra, tb], [16, 20, 4])
        else:
            f3, bm = call(functools.partial(k_b, False), "b", [u, v, w, g, r, ta, ra, tb], [16, 16])
        rb = lax.ppermute(bm, "elem", others)
        if first:
            u, v, w, g, p, dm, r, mn = call(
                functools.partial(k_c, True),
                "c1",
                [u, v, w, g, p, m, r, r3, f3, tb, rb],
                [16] * 5 + [3, 16, 4],
            )
        else:
            u, v, w, g, p, dm = call(
                functools.partial(k_c, False), "c", [u, v, w, g, p, m, r, mn, f3, tb, rb], [16] * 5 + [3]
            )
        rd = lax.ppermute(dm, "elem", mates)
        if first:
            ia, hr, rh, cp, wu, pu, wd, pd, cc, edge = call(
                k_stat, "stat", [got], [16] * 8 + [16, 5], [40, 16, 16]
            )
            statics = [ia, hr, rh, cp, cc, edge]
        p, vm = call(k_d, "d", [p, w, r, rd, wu, pu, wd, pd], [16, 16])
        rv = swap_levels(vm)
        if step < SUBSTEPS - 1:
            u, v, w, g, p, ta, tb = call(
                k_e, "e", [p, w, g, u, v, rv] + statics + [m, r], [16] * 5 + [12, 12], [16] * 4
            )
        else:
            outs = call(k_out, "out", [order, p, w, g, u, v, rv] + statics, [16] * 5, [16] * 2, free_out=True)
    return tuple(x.reshape(zonal.shape) for x in outs)


def solution(mesh):
    fields = P("lev", None, "elem")
    return jax.shard_map(
        body,
        mesh=mesh,
        in_specs=(fields,) * 6 + (P(None, "lev", "elem"), P("elem", None)),
        out_specs=(fields,) * 5,
        check_vma=False,
    )
```

```python
import functools
import math

import jax
import jax.numpy as jnp
import numpy as np
from jax import lax
from jax.experimental import pallas as pl
from jax.experimental.pallas import tpu as pltpu
from jax.sharding import PartitionSpec as P

SUBSTEPS = 3
SPEED = 0.12
DRIFT1 = 0.1
DRIFT2 = 0.06
RATE = 2.0
F32 = jnp.float32
LANES = 128
NL = 16
ORDER = (4, 3, 5, 2, 6, 1, 7, 0)
ROWS = 24


def tables():
    points = np.array([-1.0, -1.0 / math.sqrt(5.0), 1.0 / math.sqrt(5.0), 1.0])
    quad = [1.0 / 6.0, 5.0 / 6.0, 5.0 / 6.0, 1.0 / 6.0]
    d = np.zeros((4, 4))
    for t in range(4):
        for s in range(4):
            if t == s:
                d[t, s] = sum(1.0 / (points[t] - points[o]) for o in range(4) if o != t)
            else:
                top = math.prod(points[t] - points[o] for o in range(4) if o != t)
                low = math.prod(points[s] - points[o] for o in range(4) if o != s)
                d[t, s] = top / (low * (points[t] - points[s]))
    d[np.abs(d) < 1e-12] = 0.0
    return [[float(x) for x in row] for row in d], [float(a * b) for a in quad for b in quad]


D, WEIGHT = tables()


def lin(coeffs, values):
    total = None
    for c, v in zip(coeffs, values):
        if c != 0.0:
            total = c * v if total is None else total + c * v
    return total


def up(x):
    return pltpu.roll(x, LANES - 1, 1)


def down(x):
    return pltpu.roll(x, 1, 1)


def sew(row):
    last = row[3] + up(row[0])
    return [down(last), row[1], row[2], last]


def rows(ref, n):
    return ref[n * NL : (n + 1) * NL, :]


def put(ref, n, value):
    ref[n * NL : (n + 1) * NL, :] = value


def dx(get, i, j):
    return lin(D[i], [get(k * 4 + j) for k in range(4)])


def dy(get, i, j):
    return lin(D[j], [get(i * 4 + k) for k in range(4)])


def three(ref, base):
    a, b, c = (rows(ref, base + k) for k in range(3))
    return [down(c), a, b, c]


def place():
    core = lax.rem(lax.axis_index("elem"), 2)
    return core, (1 - 2 * core).astype(F32)


def inverse_of(order_ref):
    order = order_ref[...].astype(F32)
    across = jnp.broadcast_to(order, (LANES, LANES))
    along = across.T
    lane = lax.broadcasted_iota(jnp.int32, (LANES, LANES), 1).astype(F32)
    slot = lax.broadcasted_iota(jnp.int32, (LANES, LANES), 0).astype(F32)
    return jnp.sum(jnp.where(along == lane, slot, 0.0), axis=0, keepdims=True).astype(jnp.int32)


def pick(values, index):
    return jnp.take_along_axis(values, index, axis=1, mode="promise_in_bounds")


def stage_a(sg, src, p, m, r, dst, ta, tb):
    for f in range(4):
        if f < 2:
            get = functools.partial(rows, p)
        else:
            get = functools.partial(rows, src[f])
        for i in range(4):
            row = []
            for j in range(4):
                if f == 0:
                    t = (-SPEED * sg) * dx(get, i, j)
                elif f == 1:
                    t = -SPEED * dy(get, i, j)
                else:
                    t = -((DRIFT1 * sg) * dx(get, i, j) + DRIFT2 * dy(get, i, j))
                row.append(rows(m, i * 4 + j) * t)
            row = sew(row)
            for j in range(4):
                n = i * 4 + j
                own = rows(src[f], n)
                if i in (1, 2):
                    put(dst[f], n, own + rows(r, n) * row[j])
                else:
                    put(dst[f], n, own)
                    if j > 0:
                        put(ta if i == 3 else tb, f * 3 + j - 1, row[j])


def fetch(sources, targets, sem):
    copies = [pltpu.make_async_copy(a, b, sem.at[k]) for k, (a, b) in enumerate(zip(sources, targets))]
    for copy in copies:
        copy.start()
    return copies


def k_init(order, *refs):
    ins, (u, v, w, g, p, m, r, ta, tb) = refs[:6], refs[6:15]
    us, vs, ws, gs, order_s, sem = refs[15:19] + refs[25:]
    held = refs[19:25]
    copies = fetch((order,) + ins, (order_s,) + held, sem)
    core, sg = place()
    copies[0].wait()
    index = jnp.broadcast_to(inverse_of(order_s), (NL, LANES))
    for copy, src, dst in zip(copies[1:], held, (p, m, us, vs, ws, gs)):
        copy.wait()
        for i in range(4):
            for j in range(4):
                start = jnp.where(core == 1, (3 - i) * 4 + j, i * 4 + j)
                value = pick(src[pl.ds(start, NL, stride=16), :], index)
                if dst is m:
                    value = value * WEIGHT[i * 4 + j]
                put(dst, i * 4 + j, value)
    for i in range(4):
        row = sew([rows(m, i * 4 + j) for j in range(4)])
        for j in range(4):
            if i in (1, 2):
                put(r, i * 4 + j, 1.0 / row[j])
            else:
                put(r, i * 4 + j, row[j])
                if j > 0:
                    put(ta if i == 3 else tb, 12 + j - 1, row[j])
    stage_a(sg, (us, vs, ws, gs), p, m, r, (u, v, w, g), ta, tb)


def k_b(first, *refs):
    if first:
        u, v, w, g, m, r, ta, ra, tb, f3, bm, r3 = refs
        own, got = three(ta, 12), three(ra, 12)
        for j in range(4):
            put(r3, j, 1.0 / (own[j] + got[j]))
        rr = lambda j: rows(r3, j)
    else:
        u, v, w, g, r, ta, ra, tb, f3, bm = refs
        rr = lambda j: rows(r, 12 + j)
    _, sg = place()
    for f, field in enumerate((u, v, w, g)):
        own, got = three(ta, f * 3), three(ra, f * 3)
        for j in range(4):
            put(f3, f * 4 + j, rows(field, 12 + j) + rr(j) * (own[j] + got[j]))
    for j in range(4):
        along = lin(D[0], [rows(u, j), rows(u, 4 + j), rows(u, 8 + j), rows(f3, j)])
        across = dy(functools.partial(rows, v), 0, j)
        put(bm, 12 + j, sg * along + across)
    for k in range(12):
        put(bm, k, rows(tb, k))
    if first:
        for j in range(4):
            put(bm, 16 + j, rows(m, j))


def k_c(first, *refs):
    if first:
        u, v, w, g, p, m, r, r3, f3, tb, rb, uo, vo, wo, go, po, dm, ro, mo = refs
        own, got = three(tb, 12), sew([rows(rb, 16 + j) for j in range(4)])
        for j in range(4):
            put(ro, j, 1.0 / (own[j] + got[j]))
            put(ro, 12 + j, rows(r3, j))
            put(mo, j, rows(rb, 16 + j))
            for i in (1, 2):
                put(ro, i * 4 + j, rows(r, i * 4 + j))
        r, mn = ro, mo
    else:
        u, v, w, g, p, m, r, mn, f3, tb, rb, uo, vo, wo, go, po, dm = refs
    _, sg = place()
    inc = []
    for f, (field, out) in enumerate(((u, uo), (v, vo), (w, wo), (g, go))):
        own, got = three(tb, f * 3), three(rb, f * 3)
        part = []
        for j in range(4):
            add = rows(r, j) * (own[j] + got[j])
            part.append(add)
            put(out, j, rows(field, j) + add)
            put(out, 12 + j, rows(f3, f * 4 + j))
            for i in (1, 2):
                put(out, i * 4 + j, rows(field, i * 4 + j))
        if f < 2:
            inc.append(part)
    other = []
    for j in range(4):
        t = rows(rb, 12 + j) - (sg * D[0][0]) * inc[0][j] + lin(D[j], inc[1])
        other.append(rows(mn, j) * (-SPEED * t))
    other = sew(other)
    gu, gv = functools.partial(rows, uo), functools.partial(rows, vo)
    for i in range(4):
        row = sew([rows(m, i * 4 + j) * (-SPEED * (sg * dx(gu, i, j) + dy(gv, i, j))) for j in range(4)])
        for j in range(4):
            n = i * 4 + j
            total = row[j] + other[j] if i == 0 else row[j]
            put(po, n, rows(p, n) + rows(r, n) * total)
            if i == 3 and j > 0:
                put(dm, j - 1, row[j])


def level(ref, k):
    return jnp.concatenate([ref[pl.ds(k, 8, stride=32), :], ref[pl.ds(16 + k, 8, stride=32), :]], 0)


def node_of(ref, n):
    return ref[pl.ds((n % 2) * 8 + n // 2, NL, stride=16), :]


def k_d(p, w, r, rd, wu, pu, wd, pd, edge, po, vm):
    me = lax.axis_index("lev")
    got = three(rd, 0)
    for n in range(12):
        put(po, n, rows(p, n))
    for j in range(4):
        put(po, 12 + j, rows(p, 12 + j) + rows(r, 12 + j) * got[j])
    su = sd = None
    for k in range(NL):
        wk, pk = level(w, k), level(po, k)
        a = rows(wu, k) * wk + rows(pu, k) * pk
        b = rows(wd, k) * wk + rows(pd, k) * pk
        su = a if su is None else su + a
        sd = b if sd is None else sd + b
    low, high = level(po, 0), level(po, NL - 1)
    su_far = su + rows(edge, 6) * high
    sd_far = sd - rows(edge, 5) * low
    for k, c in enumerate(ORDER):
        above = c > me
        total = jnp.where(above, jnp.where(c > me + 1, su_far, su), jnp.where(c < me - 1, sd_far, sd))
        vm[k * 32 : k * 32 + 16, :] = total
        vm[k * 32 + 16 : k * 32 + 32, :] = jnp.where(above, high, low)


def solve(p, w, rv, ia, hr, rh, cp, edge, s_out, p_out):
    me = lax.axis_index("lev")
    low, high = level(p, 0), level(p, NL - 1)
    from_below = from_above = prev = then = jnp.zeros_like(low)
    for k, c in enumerate(ORDER):
        part, side = rows(rv, 2 * k), rows(rv, 2 * k + 1)
        from_below = from_below + jnp.where(c < me, part, 0.0)
        from_above = from_above + jnp.where(c > me, part, 0.0)
        prev = jnp.where(c == me - 1, side, prev)
        then = jnp.where(c == me + 1, side, then)
    from_below = from_below * rows(edge, 7) - rows(edge, 0) * low
    from_above = from_above * rows(edge, 8) + rows(edge, 1) * high
    d = []
    last = from_below
    for k in range(NL):
        below = level(p, k - 1) if k > 0 else prev
        above = level(p, k + 1) if k < NL - 1 else then
        q = level(w, k) * rows(ia, k) - (above - below) * rows(hr, k)
        last = rows(cp, k) * (q + last)
        d.append(last)
    s = (d[NL - 1] + rows(cp, NL - 1) * from_above) * rows(edge, 2)
    after = from_above + rows(edge, 4) * s
    for k in range(NL - 1, -1, -1):
        put(s_out, k, s)
        if k > 0:
            nxt = d[k - 1] + rows(cp, k - 1) * s
        else:
            nxt = from_below + rows(edge, 3) * s
        put(p_out, k, level(p, k) - rows(rh, k) * (after - nxt))
        after, s = s, nxt


def k_e(p, w, g, u, v, rv, ia, hr, rh, cp, edge, m, r, uo, vo, wo, go, po, ta, tb, ss, ps, ws, gs):
    _, sg = place()
    solve(p, w, rv, ia, hr, rh, cp, edge, ss, ps)
    for n in range(16):
        s = node_of(ss, n)
        put(ws, n, s)
        put(gs, n, rows(g, n) + RATE * s)
        put(po, n, node_of(ps, n))
    stage_a(sg, (u, v, ws, gs), po, m, r, (uo, vo, wo, go), ta, tb)


def k_out(order, p, w, g, u, v, rv, ia, hr, rh, cp, edge, uo, vo, wo, po, go, ss, ps):
    core, _ = place()
    solve(p, w, rv, ia, hr, rh, cp, edge, ss, ps)
    index = jnp.broadcast_to(order[...], (NL, LANES))
    for i in range(4):
        for j in range(4):
            n = i * 4 + j
            start = jnp.where(core == 1, (3 - i) * 4 + j, n)
            s = node_of(ss, n)
            for out, value in (
                (uo, rows(u, n)),
                (vo, rows(v, n)),
                (wo, s),
                (po, node_of(ps, n)),
                (go, rows(g, n) + RATE * s),
            ):
                out[pl.ds(start, NL, stride=16), :] = pick(value, index)


def k_col(order, st_in, out, a_s, ia_s, st, order_s, sem):
    copies = fetch((order, st_in), (order_s, st), sem)
    for copy in copies:
        copy.wait()
    index = jnp.broadcast_to(inverse_of(order_s), (NL, LANES))
    for k in range(16):
        a = pick(st[k * 16 : k * 16 + 16, :], index)
        a_s[k * 16 : k * 16 + 16, :] = a
        ia_s[k * 16 : k * 16 + 16, :] = 1.0 / a
    one = jnp.ones((2, LANES), F32)
    zero = jnp.zeros((2, LANES), F32)
    pair = lambda ref, k: ref[2 * k : 2 * k + 2, :]
    th, de = one, one
    below, rho = [one], [one]
    for k in range(128):
        de = de + th * pair(ia_s, k)
        th = th + de
        if k % 16 == 15:
            below.append(th)
            rho.append(de / th)
    ps, de = one, one
    above, sig = [one] * 9, [one] * 9
    for k in range(127, -1, -1):
        de = de + ps * pair(ia_s, k)
        ps = ps + de
        if k % 16 == 0:
            above[k // 16] = ps
            sig[k // 16] = de / ps
    half = lambda k: 0.5 * jnp.sqrt(pair(ia_s, k)) if 0 <= k < 128 else zero
    for place_of, b in enumerate(ORDER):
        tail = [rho[b], sig[b + 1], half(16 * b - 1), half(16 * b + 16), below[b], above[b + 1], zero, zero]
        for t in range(ROWS):
            start = (place_of * ROWS + t) * 2
            out[start : start + 2, :] = pair(a_s, b * 16 + t) if t < 16 else tail[t - 16]


def k_stat(got, ia, hr, rh, cp, wu, pu, wd, pd, edge, scr, tu_s, td_s):
    core, _ = place()
    size = 2 * ROWS
    for k, src in enumerate(ORDER):
        goal = jnp.where(core == 1, src ^ 6, src)
        scr[pl.ds(pl.multiple_of(goal * size, 8), size), :] = got[k * size : (k + 1) * size, :]

    def row(t):
        return jnp.concatenate([scr[pl.ds(2 * t + e, 8, stride=2 * ROWS), :] for e in range(2)], 0)

    for k in range(NL):
        a = row(k)
        ra = 1.0 / a
        root = jnp.sqrt(a)
        put(ia, k, ra)
        put(rh, k, 0.5 * root)
        put(hr, k, 0.5 * (ra * root))
    rho, sig, h_lo, h_hi, th0, ps0 = (row(16 + t) for t in range(6))
    th, de = th0, rho * th0
    for k in range(NL):
        de = de + th * rows(ia, k)
        new = th + de
        put(cp, k, th / new)
        put(tu_s, k, th)
        th = new
    ps, de = ps0, sig * ps0
    for k in range(NL - 1, -1, -1):
        de = de + ps * rows(ia, k)
        put(td_s, k, ps)
        ps = ps + de
    cpm, cqp = 1.0 - rho, 1.0 - sig
    for ref, wt, pt, in ((tu_s, wu, pu), (td_s, wd, pd)):
        for k in range(NL):
            put(wt, k, rows(ref, k) * rows(ia, k))
            value = None
            if k < NL - 1:
                value = rows(ref, k + 1) * rows(hr, k + 1)
            elif ref is td_s:
                value = rows(ref, k) * cqp * h_hi
            else:
                value = jnp.zeros_like(rho)
            if k > 0:
                value = value - rows(ref, k - 1) * rows(hr, k - 1)
            elif ref is tu_s:
                value = value - rows(ref, 0) * cpm * h_lo
            put(pt, k, value)
    put(edge, 0, cpm * h_lo)
    put(edge, 1, cqp * h_hi)
    put(edge, 2, 1.0 / (1.0 - rows(cp, NL - 1) * cqp))
    put(edge, 3, cpm)
    put(edge, 4, cqp)
    put(edge, 5, ps * h_lo)
    put(edge, 6, th * h_hi)
    put(edge, 7, 1.0 / th0)
    put(edge, 8, 1.0 / ps0)


def call(kernel, name, args, outs, scratch=(), hbm_in=0, free_out=False):
    vmem = pl.BlockSpec(memory_space=pltpu.VMEM)
    hbm = pl.BlockSpec(memory_space=pl.ANY)
    args = [
        pltpu.with_memory_space_constraint(x, pltpu.HBM if k < hbm_in else pltpu.VMEM) if k < hbm_in or x.dtype == F32 else x
        for k, x in enumerate(args)
    ]
    kind = jax.ShapeDtypeStruct if free_out else pltpu.VMEM
    spare = [pltpu.VMEM((n * NL, LANES), F32) for n in scratch]
    if hbm_in:
        spare += [pltpu.VMEM((1, LANES), jnp.int32), pltpu.SemaphoreType.DMA((hbm_in,))]
    return pl.pallas_call(
        kernel,
        out_shape=[kind((n * NL, LANES), F32) for n in outs],
        in_specs=[hbm if k < hbm_in else vmem for k in range(len(args))],
        out_specs=[vmem] * len(outs),
        scratch_shapes=spare,
        compiler_params=pltpu.CompilerParams(vmem_limit_bytes=8 << 20),
        name=name,
    )(*args)


def body(zonal, meridional, vertical, pressure, geopotential, layer_mass, stiffness, order):
    count = lax.axis_size("elem")
    mates = [(i, i ^ 1) for i in range(count)]
    others = [(i, (i + 1) % count if i % 2 else (i - 1) % count) for i in range(count)]
    flat = lambda x: x.reshape(-1, LANES)
    u, v, w, p, g, lm = (flat(x) for x in (zonal, meridional, vertical, pressure, geopotential, layer_mass))

    def swap_levels(x):
        return lax.all_to_all(x.reshape(8, -1, LANES), "lev", 0, 0, tiled=True, axis_index_groups=[list(ORDER)]).reshape(-1, LANES)

    (sent,) = call(k_col, "col", [order, flat(stiffness)], [ROWS], [16, 16, 16], hbm_in=2)
    got = swap_levels(sent)
    u, v, w, g, p, m, r, ta, tb = call(
        k_init, "init", [order, p, lm, u, v, w, g], [16] * 7 + [15, 15], [16] * 10, hbm_in=7
    )
    mn = r3 = None
    statics = None
    for step in range(SUBSTEPS):
        first = step == 0
        ra = lax.ppermute(ta, "elem", mates)
        if first:
            f3, bm, r3 = call(functools.partial(k_b, True), "b1", [u, v, w, g, m, r, ta, ra, tb], [16, 20, 4])
        else:
            f3, bm = call(functools.partial(k_b, False), "b", [u, v, w, g, r, ta, ra, tb], [16, 16])
        rb = lax.ppermute(bm, "elem", others)
        if first:
            u, v, w, g, p, dm, r, mn = call(
                functools.partial(k_c, True),
                "c1",
                [u, v, w, g, p, m, r, r3, f3, tb, rb],
                [16] * 5 + [3, 16, 4],
            )
        else:
            u, v, w, g, p, dm = call(
                functools.partial(k_c, False), "c", [u, v, w, g, p, m, r, mn, f3, tb, rb], [16] * 5 + [3]
            )
        rd = lax.ppermute(dm, "elem", mates)
        if first:
            ia, hr, rh, cp, wu, pu, wd, pd, edge = call(
                k_stat, "stat", [got], [16] * 8 + [9], [ROWS, 16, 16]
            )
            statics = [ia, hr, rh, cp, edge]
        p, vm = call(k_d, "d", [p, w, r, rd, wu, pu, wd, pd, edge], [16, 16])
        rv = swap_levels(vm)
        if step < SUBSTEPS - 1:
            u, v, w, g, p, ta, tb = call(
                k_e, "e", [p, w, g, u, v, rv] + statics + [m, r], [16] * 5 + [12, 12], [16] * 4
            )
        else:
            outs = call(k_out, "out", [order, p, w, g, u, v, rv] + statics, [16] * 5, [16] * 2, free_out=True)
    return tuple(x.reshape(zonal.shape) for x in outs)


def solution(mesh):
    fields = P("lev", None, "elem")
    return jax.shard_map(
        body,
        mesh=mesh,
        in_specs=(fields,) * 6 + (P(None, "lev", "elem"), P("elem", None)),
        out_specs=(fields,) * 5,
        check_vma=False,
    )
```

```python
import functools
import math

import jax
import jax.numpy as jnp
import numpy as np
from jax import lax
from jax.experimental import pallas as pl
from jax.experimental.pallas import tpu as pltpu
from jax.sharding import PartitionSpec as P

SUBSTEPS = 3
SPEED = 0.12
DRIFT1 = 0.1
DRIFT2 = 0.06
RATE = 2.0
F32 = jnp.float32
LANES = 128
NL = 16
ORDER = (4, 0, 7, 1, 6, 2, 5, 3)
LONG = 64
ROWS = 24


def tables():
    points = np.array([-1.0, -1.0 / math.sqrt(5.0), 1.0 / math.sqrt(5.0), 1.0])
    quad = [1.0 / 6.0, 5.0 / 6.0, 5.0 / 6.0, 1.0 / 6.0]
    d = np.zeros((4, 4))
    for t in range(4):
        for s in range(4):
            if t == s:
                d[t, s] = sum(1.0 / (points[t] - points[o]) for o in range(4) if o != t)
            else:
                top = math.prod(points[t] - points[o] for o in range(4) if o != t)
                low = math.prod(points[s] - points[o] for o in range(4) if o != s)
                d[t, s] = top / (low * (points[t] - points[s]))
    d[np.abs(d) < 1e-12] = 0.0
    return [[float(x) for x in row] for row in d], [float(a * b) for a in quad for b in quad]


D, WEIGHT = tables()


def lin(coeffs, values):
    total = None
    for c, v in zip(coeffs, values):
        if c != 0.0:
            total = c * v if total is None else total + c * v
    return total


def up(x):
    return pltpu.roll(x, LANES - 1, 1)


def down(x):
    return pltpu.roll(x, 1, 1)


def sew(row):
    last = row[3] + up(row[0])
    return [down(last), row[1], row[2], last]


def rows(ref, n):
    return ref[n * NL : (n + 1) * NL, :]


def put(ref, n, value):
    ref[n * NL : (n + 1) * NL, :] = value


def dx(get, i, j):
    return lin(D[i], [get(k * 4 + j) for k in range(4)])


def dy(get, i, j):
    return lin(D[j], [get(i * 4 + k) for k in range(4)])


def three(ref, base):
    a, b, c = (rows(ref, base + k) for k in range(3))
    return [down(c), a, b, c]


def place():
    core = lax.rem(lax.axis_index("elem"), 2)
    return core, (1 - 2 * core).astype(F32)


def inverse_of(order_ref):
    order = order_ref[...].astype(F32)
    across = jnp.broadcast_to(order, (LANES, LANES))
    along = across.T
    lane = lax.broadcasted_iota(jnp.int32, (LANES, LANES), 1).astype(F32)
    slot = lax.broadcasted_iota(jnp.int32, (LANES, LANES), 0).astype(F32)
    return jnp.sum(jnp.where(along == lane, slot, 0.0), axis=0, keepdims=True).astype(jnp.int32)


def pick(values, index):
    return jnp.take_along_axis(values, index, axis=1, mode="promise_in_bounds")


def stage_a(sg, src, p, m, r, dst, ta, tb):
    for f in range(4):
        if f < 2:
            get = functools.partial(rows, p)
        else:
            get = functools.partial(rows, src[f])
        for i in range(4):
            row = []
            for j in range(4):
                if f == 0:
                    t = (-SPEED * sg) * dx(get, i, j)
                elif f == 1:
                    t = -SPEED * dy(get, i, j)
                else:
                    t = -((DRIFT1 * sg) * dx(get, i, j) + DRIFT2 * dy(get, i, j))
                row.append(rows(m, i * 4 + j) * t)
            row = sew(row)
            for j in range(4):
                n = i * 4 + j
                own = rows(src[f], n)
                if i in (1, 2):
                    put(dst[f], n, own + rows(r, n) * row[j])
                else:
                    put(dst[f], n, own)
                    if j > 0:
                        put(ta if i == 3 else tb, f * 3 + j - 1, row[j])


def fetch(sources, targets, sem):
    copies = [pltpu.make_async_copy(a, b, sem.at[k]) for k, (a, b) in enumerate(zip(sources, targets))]
    for copy in copies:
        copy.start()
    return copies


def k_init(order, *refs):
    ins, (u, v, w, g, p, m, r, ta, tb) = refs[:6], refs[6:15]
    us, vs, ws, gs, order_s, sem = refs[15:19] + refs[25:]
    held = refs[19:25]
    copies = fetch((order,) + ins, (order_s,) + held, sem)
    core, sg = place()
    copies[0].wait()
    index = jnp.broadcast_to(inverse_of(order_s), (NL, LANES))
    for copy, src, dst in zip(copies[1:], held, (p, m, us, vs, ws, gs)):
        copy.wait()
        for i in range(4):
            for j in range(4):
                start = jnp.where(core == 1, (3 - i) * 4 + j, i * 4 + j)
                value = pick(src[pl.ds(start, NL, stride=16), :], index)
                if dst is m:
                    value = value * WEIGHT[i * 4 + j]
                put(dst, i * 4 + j, value)
    for i in range(4):
        row = sew([rows(m, i * 4 + j) for j in range(4)])
        for j in range(4):
            if i in (1, 2):
                put(r, i * 4 + j, 1.0 / row[j])
            else:
                put(r, i * 4 + j, row[j])
                if j > 0:
                    put(ta if i == 3 else tb, 12 + j - 1, row[j])
    stage_a(sg, (us, vs, ws, gs), p, m, r, (u, v, w, g), ta, tb)


def k_b(first, *refs):
    if first:
        u, v, w, g, m, r, ta, ra, tb, f3, bm, r3 = refs
        own, got = three(ta, 12), three(ra, 12)
        for j in range(4):
            put(r3, j, 1.0 / (own[j] + got[j]))
        rr = lambda j: rows(r3, j)
    else:
        u, v, w, g, r, ta, ra, tb, f3, bm = refs
        rr = lambda j: rows(r, 12 + j)
    _, sg = place()
    for f, field in enumerate((u, v, w, g)):
        own, got = three(ta, f * 3), three(ra, f * 3)
        for j in range(4):
            put(f3, f * 4 + j, rows(field, 12 + j) + rr(j) * (own[j] + got[j]))
    for j in range(4):
        along = lin(D[0], [rows(u, j), rows(u, 4 + j), rows(u, 8 + j), rows(f3, j)])
        across = dy(functools.partial(rows, v), 0, j)
        put(bm, 12 + j, sg * along + across)
    for k in range(12):
        put(bm, k, rows(tb, k))
    if first:
        for j in range(4):
            put(bm, 16 + j, rows(m, j))


def k_c(first, *refs):
    if first:
        u, v, w, g, p, m, r, r3, f3, tb, rb, uo, vo, wo, go, po, dm, ro, mo = refs
        own, got = three(tb, 12), sew([rows(rb, 16 + j) for j in range(4)])
        for j in range(4):
            put(ro, j, 1.0 / (own[j] + got[j]))
            put(ro, 12 + j, rows(r3, j))
            put(mo, j, rows(rb, 16 + j))
            for i in (1, 2):
                put(ro, i * 4 + j, rows(r, i * 4 + j))
        r, mn = ro, mo
    else:
        u, v, w, g, p, m, r, mn, f3, tb, rb, uo, vo, wo, go, po, dm = refs
    _, sg = place()
    inc = []
    for f, (field, out) in enumerate(((u, uo), (v, vo), (w, wo), (g, go))):
        own, got = three(tb, f * 3), three(rb, f * 3)
        part = []
        for j in range(4):
            add = rows(r, j) * (own[j] + got[j])
            part.append(add)
            put(out, j, rows(field, j) + add)
            put(out, 12 + j, rows(f3, f * 4 + j))
            for i in (1, 2):
                put(out, i * 4 + j, rows(field, i * 4 + j))
        if f < 2:
            inc.append(part)
    other = []
    for j in range(4):
        t = rows(rb, 12 + j) - (sg * D[0][0]) * inc[0][j] + lin(D[j], inc[1])
        other.append(rows(mn, j) * (-SPEED * t))
    other = sew(other)
    gu, gv = functools.partial(rows, uo), functools.partial(rows, vo)
    for i in range(4):
        row = sew([rows(m, i * 4 + j) * (-SPEED * (sg * dx(gu, i, j) + dy(gv, i, j))) for j in range(4)])
        for j in range(4):
            n = i * 4 + j
            total = row[j] + other[j] if i == 0 else row[j]
            put(po, n, rows(p, n) + rows(r, n) * total)
            if i == 3 and j > 0:
                put(dm, j - 1, row[j])


def level(ref, k):
    return jnp.concatenate([ref[pl.ds(k, 8, stride=32), :], ref[pl.ds(16 + k, 8, stride=32), :]], 0)


def node_of(ref, n):
    return ref[pl.ds((n % 2) * 8 + n // 2, NL, stride=16), :]


def k_d(p, w, r, rd, wu, pu, wd, pd, edge, po, vm):
    me = lax.axis_index("lev")
    got = three(rd, 0)
    for n in range(12):
        put(po, n, rows(p, n))
    for j in range(4):
        put(po, 12 + j, rows(p, 12 + j) + rows(r, 12 + j) * got[j])
    su = sd = None
    for k in range(NL):
        wk, pk = level(w, k), level(po, k)
        a = rows(wu, k) * wk + rows(pu, k) * pk
        b = rows(wd, k) * wk + rows(pd, k) * pk
        su = a if su is None else su + a
        sd = b if sd is None else sd + b
    low, high = level(po, 0), level(po, NL - 1)
    su_far = su + rows(edge, 6) * high
    sd_far = sd - rows(edge, 5) * low
    for k, c in enumerate(ORDER):
        above = c > me
        total = jnp.where(above, jnp.where(c > me + 1, su_far, su), jnp.where(c < me - 1, sd_far, sd))
        vm[k * 32 : k * 32 + 16, :] = total
        vm[k * 32 + 16 : k * 32 + 32, :] = jnp.where(above, high, low)


def solve(p, w, rv, ia, hr, rh, cp, edge, s_out, p_out):
    me = lax.axis_index("lev")
    low, high = level(p, 0), level(p, NL - 1)
    from_below = from_above = prev = then = jnp.zeros_like(low)
    for k, c in enumerate(ORDER):
        part, side = rows(rv, 2 * k), rows(rv, 2 * k + 1)
        from_below = from_below + jnp.where(c < me, part, 0.0)
        from_above = from_above + jnp.where(c > me, part, 0.0)
        prev = jnp.where(c == me - 1, side, prev)
        then = jnp.where(c == me + 1, side, then)
    from_below = from_below * rows(edge, 7) - rows(edge, 0) * low
    from_above = from_above * rows(edge, 8) + rows(edge, 1) * high
    d = []
    last = from_below
    for k in range(NL):
        below = level(p, k - 1) if k > 0 else prev
        above = level(p, k + 1) if k < NL - 1 else then
        q = level(w, k) * rows(ia, k) - (above - below) * rows(hr, k)
        last = rows(cp, k) * (q + last)
        d.append(last)
    s = (d[NL - 1] + rows(cp, NL - 1) * from_above) * rows(edge, 2)
    after = from_above + rows(edge, 4) * s
    for k in range(NL - 1, -1, -1):
        put(s_out, k, s)
        if k > 0:
            nxt = d[k - 1] + rows(cp, k - 1) * s
        else:
            nxt = from_below + rows(edge, 3) * s
        put(p_out, k, level(p, k) - rows(rh, k) * (after - nxt))
        after, s = s, nxt


def k_e(p, w, g, u, v, rv, ia, hr, rh, cp, edge, m, r, uo, vo, wo, go, po, ta, tb, ss, ps, ws, gs):
    _, sg = place()
    solve(p, w, rv, ia, hr, rh, cp, edge, ss, ps)
    for n in range(16):
        s = node_of(ss, n)
        put(ws, n, s)
        put(gs, n, rows(g, n) + RATE * s)
        put(po, n, node_of(ps, n))
    stage_a(sg, (u, v, ws, gs), po, m, r, (uo, vo, wo, go), ta, tb)


def k_out(order, p, w, g, u, v, rv, ia, hr, rh, cp, edge, uo, vo, wo, po, go, ss, ps, us, vs, ws, qs, gs, order_s, sem):
    core, _ = place()
    (copy,) = fetch((order,), (order_s,), sem)
    copy.wait()
    index = jnp.broadcast_to(order_s[...], (NL, LANES))

    def store(value_of, held, out, k):
        for n in range(16):
            start = jnp.where(core == 1, (3 - n // 4) * 4 + n % 4, n)
            held[pl.ds(start, NL, stride=16), :] = pick(value_of(n), index)
        copy = pltpu.make_async_copy(held, out, sem.at[k])
        copy.start()
        return copy

    copies = [
        store(functools.partial(rows, u), us, uo, 1),
        store(functools.partial(rows, v), vs, vo, 2),
    ]
    solve(p, w, rv, ia, hr, rh, cp, edge, ss, ps)
    copies += [
        store(functools.partial(node_of, ss), ws, wo, 3),
        store(functools.partial(node_of, ps), qs, po, 4),
        store(lambda n: rows(g, n) + RATE * node_of(ss, n), gs, go, 5),
    ]
    for copy in copies:
        copy.wait()


def k_col(order, st_in, after, out, a_s, ia_s, st, order_s, sem):
    copies = fetch((order, st_in), (order_s, st), sem)
    for copy in copies:
        copy.wait()
    index = jnp.broadcast_to(inverse_of(order_s), (NL, LANES))
    for k in range(16):
        a = pick(st[k * 16 : k * 16 + 16, :], index)
        a_s[k * 16 : k * 16 + 16, :] = a
        ia_s[k * 16 : k * 16 + 16, :] = 1.0 / a
    one = jnp.ones((2, LANES), F32)
    zero = jnp.zeros((2, LANES), F32)
    pair = lambda ref, k: ref[2 * k : 2 * k + 2, :]
    th, de = one, one
    below, rho = [one], [one]
    for k in range(128):
        de = de + th * pair(ia_s, k)
        th = th + de
        if k % 16 == 15:
            below.append(th)
            rho.append(de / th)
    ps, de = one, one
    above, sig = [one] * 9, [one] * 9
    for k in range(127, -1, -1):
        de = de + ps * pair(ia_s, k)
        ps = ps + de
        if k % 16 == 0:
            above[k // 16] = ps
            sig[k // 16] = de / ps
    half = lambda k: 0.5 * jnp.sqrt(pair(ia_s, k)) if 0 <= k < 128 else zero
    for place_of, b in enumerate(ORDER):
        tail = [rho[b], sig[b + 1], half(16 * b - 1), half(16 * b + 16), below[b], above[b + 1], zero, zero]
        for t in range(ROWS):
            start = (place_of * ROWS + t) * 2
            out[start : start + 2, :] = pair(a_s, b * 16 + t) if t < 16 else tail[t - 16]


def k_stat(got, after, ia, hr, rh, cp, wu, pu, wd, pd, edge, scr, tu_s, td_s):
    core, _ = place()
    size = 2 * ROWS
    for k, src in enumerate(ORDER):
        goal = jnp.where(core == 1, src ^ 6, src)
        scr[pl.ds(pl.multiple_of(goal * size, 8), size), :] = got[k * size : (k + 1) * size, :]

    def row(t):
        return jnp.concatenate([scr[pl.ds(2 * t + e, 8, stride=2 * ROWS), :] for e in range(2)], 0)

    for k in range(NL):
        a = row(k)
        ra = 1.0 / a
        root = jnp.sqrt(a)
        put(ia, k, ra)
        put(rh, k, 0.5 * root)
        put(hr, k, 0.5 * (ra * root))
    rho, sig, h_lo, h_hi, th0, ps0 = (row(16 + t) for t in range(6))
    th, de = th0, rho * th0
    for k in range(NL):
        de = de + th * rows(ia, k)
        new = th + de
        put(cp, k, th / new)
        put(tu_s, k, th)
        th = new
    ps, de = ps0, sig * ps0
    for k in range(NL - 1, -1, -1):
        de = de + ps * rows(ia, k)
        put(td_s, k, ps)
        ps = ps + de
    cpm, cqp = 1.0 - rho, 1.0 - sig
    for ref, wt, pt, in ((tu_s, wu, pu), (td_s, wd, pd)):
        for k in range(NL):
            put(wt, k, rows(ref, k) * rows(ia, k))
            value = None
            if k < NL - 1:
                value = rows(ref, k + 1) * rows(hr, k + 1)
            elif ref is td_s:
                value = rows(ref, k) * cqp * h_hi
            else:
                value = jnp.zeros_like(rho)
            if k > 0:
                value = value - rows(ref, k - 1) * rows(hr, k - 1)
            elif ref is tu_s:
                value = value - rows(ref, 0) * cpm * h_lo
            put(pt, k, value)
    put(edge, 0, cpm * h_lo)
    put(edge, 1, cqp * h_hi)
    put(edge, 2, 1.0 / (1.0 - rows(cp, NL - 1) * cqp))
    put(edge, 3, cpm)
    put(edge, 4, cqp)
    put(edge, 5, ps * h_lo)
    put(edge, 6, th * h_hi)
    put(edge, 7, 1.0 / th0)
    put(edge, 8, 1.0 / ps0)


def call(kernel, name, args, outs, scratch=(), hbm_in=0, free_out=False):
    vmem = pl.BlockSpec(memory_space=pltpu.VMEM)
    hbm = pl.BlockSpec(memory_space=pl.ANY)
    args = [
        pltpu.with_memory_space_constraint(x, pltpu.HBM if k < hbm_in else pltpu.VMEM) if k < hbm_in or x.dtype == F32 else x
        for k, x in enumerate(args)
    ]
    kind = jax.ShapeDtypeStruct if free_out else pltpu.VMEM
    spare = [pltpu.VMEM((n * NL, LANES), F32) for n in scratch]
    if hbm_in:
        spare += [pltpu.VMEM((1, LANES), jnp.int32), pltpu.SemaphoreType.DMA((8,))]
    return pl.pallas_call(
        kernel,
        out_shape=[kind((n * NL, LANES), F32) for n in outs],
        in_specs=[hbm if k < hbm_in else vmem for k in range(len(args))],
        out_specs=[hbm if free_out else vmem] * len(outs),
        scratch_shapes=spare,
        compiler_params=pltpu.CompilerParams(vmem_limit_bytes=8 << 20),
        name=name,
    )(*args)


def body(zonal, meridional, vertical, pressure, geopotential, layer_mass, stiffness, order):
    count = lax.axis_size("elem")
    mates = [(i, i ^ 1) for i in range(count)]
    others = [(i, (i + 1) % count if i % 2 else (i - 1) % count) for i in range(count)]
    flat = lambda x: x.reshape(-1, LANES)
    u, v, w, p, g, lm = (flat(x) for x in (zonal, meridional, vertical, pressure, geopotential, layer_mass))

    def swap_levels(x):
        return lax.all_to_all(x.reshape(8, -1, LANES), "lev", 0, 0, tiled=True, axis_index_groups=[list(ORDER)]).reshape(-1, LANES)

    u, v, w, g, p, m, r, ta, tb = call(
        k_init, "init", [order, p, lm, u, v, w, g], [16] * 7 + [15, 15], [16] * 10, hbm_in=7
    )
    mn = r3 = None
    statics = None
    for step in range(SUBSTEPS):
        first = step == 0
        ra = lax.ppermute(ta, "elem", mates)
        if first:
            f3, bm, r3 = call(functools.partial(k_b, True), "b1", [u, v, w, g, m, r, ta, ra, tb], [16, 20, 4])
        else:
            f3, bm = call(functools.partial(k_b, False), "b", [u, v, w, g, r, ta, ra, tb], [16, 16])
        rb = lax.ppermute(bm, "elem", others)
        if first:
            (sent,) = call(k_col, "col", [order, flat(stiffness), bm], [ROWS], [16, 16, 16], hbm_in=2)
            got = swap_levels(sent)
        if first:
            u, v, w, g, p, dm, r, mn = call(
                functools.partial(k_c, True),
                "c1",
                [u, v, w, g, p, m, r, r3, f3, tb, rb],
                [16] * 5 + [LONG, 16, 4],
            )
        else:
            u, v, w, g, p, dm = call(
                functools.partial(k_c, False), "c", [u, v, w, g, p, m, r, mn, f3, tb, rb], [16] * 5 + [3]
            )
        rd = lax.ppermute(dm, "elem", mates)
        if first:
            ia, hr, rh, cp, wu, pu, wd, pd, edge = call(
                k_stat, "stat", [got, rd], [16] * 8 + [9], [ROWS, 16, 16]
            )
            statics = [ia, hr, rh, cp, edge]
        p, vm = call(k_d, "d", [p, w, r, rd, wu, pu, wd, pd, edge], [16, 16])
        rv = swap_levels(vm)
        if step < SUBSTEPS - 1:
            u, v, w, g, p, ta, tb = call(
                k_e, "e", [p, w, g, u, v, rv] + statics + [m, r], [16] * 5 + [12, 12], [16] * 4
            )
        else:
            outs = call(k_out, "out", [order, p, w, g, u, v, rv] + statics, [16] * 5, [16] * 7, hbm_in=1, free_out=True)
    return tuple(x.reshape(zonal.shape) for x in outs)


def solution(mesh):
    fields = P("lev", None, "elem")
    return jax.shard_map(
        body,
        mesh=mesh,
        in_specs=(fields,) * 6 + (P(None, "lev", "elem"), P("elem", None)),
        out_specs=(fields,) * 5,
        check_vma=False,
    )
```

```python
import functools
import math

import jax
import jax.numpy as jnp
import numpy as np
from jax import lax
from jax.experimental import pallas as pl
from jax.experimental.pallas import tpu as pltpu
from jax.sharding import PartitionSpec as P

SUBSTEPS = 3
SPEED = 0.12
DRIFT1 = 0.1
DRIFT2 = 0.06
RATE = 2.0
F32 = jnp.float32
LANES = 128
NL = 16
ORDER = (4, 0, 7, 1, 6, 2, 5, 3)
LONG = 72
ROWS = 24


def tables():
    points = np.array([-1.0, -1.0 / math.sqrt(5.0), 1.0 / math.sqrt(5.0), 1.0])
    quad = [1.0 / 6.0, 5.0 / 6.0, 5.0 / 6.0, 1.0 / 6.0]
    d = np.zeros((4, 4))
    for t in range(4):
        for s in range(4):
            if t == s:
                d[t, s] = sum(1.0 / (points[t] - points[o]) for o in range(4) if o != t)
            else:
                top = math.prod(points[t] - points[o] for o in range(4) if o != t)
                low = math.prod(points[s] - points[o] for o in range(4) if o != s)
                d[t, s] = top / (low * (points[t] - points[s]))
    d[np.abs(d) < 1e-12] = 0.0
    return [[float(x) for x in row] for row in d], [float(a * b) for a in quad for b in quad]


D, WEIGHT = tables()


def lin(coeffs, values):
    total = None
    for c, v in zip(coeffs, values):
        if c != 0.0:
            total = c * v if total is None else total + c * v
    return total


def up(x):
    return pltpu.roll(x, LANES - 1, 1)


def down(x):
    return pltpu.roll(x, 1, 1)


def sew(row):
    last = row[3] + up(row[0])
    return [down(last), row[1], row[2], last]


def rows(ref, n):
    return ref[n * NL : (n + 1) * NL, :]


def put(ref, n, value):
    ref[n * NL : (n + 1) * NL, :] = value


def dx(get, i, j):
    return lin(D[i], [get(k * 4 + j) for k in range(4)])


def dy(get, i, j):
    return lin(D[j], [get(i * 4 + k) for k in range(4)])


def three(ref, base):
    a, b, c = (rows(ref, base + k) for k in range(3))
    return [down(c), a, b, c]


def place():
    core = lax.rem(lax.axis_index("elem"), 2)
    return core, (1 - 2 * core).astype(F32)


def inverse_of(order_ref):
    order = order_ref[...].astype(F32)
    across = jnp.broadcast_to(order, (LANES, LANES))
    along = across.T
    lane = lax.broadcasted_iota(jnp.int32, (LANES, LANES), 1).astype(F32)
    slot = lax.broadcasted_iota(jnp.int32, (LANES, LANES), 0).astype(F32)
    return jnp.sum(jnp.where(along == lane, slot, 0.0), axis=0, keepdims=True).astype(jnp.int32)


def pick(values, index):
    return jnp.take_along_axis(values, index, axis=1, mode="promise_in_bounds")


def stage_a(sg, src, p, m, r, dst, ta, tb):
    for f in range(4):
        if f < 2:
            get = functools.partial(rows, p)
        else:
            get = functools.partial(rows, src[f])
        for i in range(4):
            row = []
            for j in range(4):
                if f == 0:
                    t = (-SPEED * sg) * dx(get, i, j)
                elif f == 1:
                    t = -SPEED * dy(get, i, j)
                else:
                    t = -((DRIFT1 * sg) * dx(get, i, j) + DRIFT2 * dy(get, i, j))
                row.append(rows(m, i * 4 + j) * t)
            row = sew(row)
            for j in range(4):
                n = i * 4 + j
                own = rows(src[f], n)
                if i in (1, 2):
                    put(dst[f], n, own + rows(r, n) * row[j])
                else:
                    put(dst[f], n, own)
                    if j > 0:
                        put(ta if i == 3 else tb, f * 3 + j - 1, row[j])


def fetch(sources, targets, sem):
    copies = [pltpu.make_async_copy(a, b, sem.at[k]) for k, (a, b) in enumerate(zip(sources, targets))]
    for copy in copies:
        copy.start()
    return copies


def k_init(order, *refs):
    ins, (u, v, w, g, p, m, r, ta, tb, st, index_out) = refs[:7], refs[7:18]
    us, vs, ws, gs, order_s, sem = refs[18:22] + refs[28:]
    held = refs[22:28]
    copies = fetch((order,) + ins, (order_s,) + held + (st,), sem)
    core, sg = place()
    copies[0].wait()
    inverse = inverse_of(order_s)
    index_out[...] = inverse
    index = jnp.broadcast_to(inverse, (NL, LANES))
    for copy, src, dst in zip(copies[1:7], held, (p, m, us, vs, ws, gs)):
        copy.wait()
        for i in range(4):
            for j in range(4):
                start = jnp.where(core == 1, (3 - i) * 4 + j, i * 4 + j)
                value = pick(src[pl.ds(start, NL, stride=16), :], index)
                if dst is m:
                    value = value * WEIGHT[i * 4 + j]
                put(dst, i * 4 + j, value)
    for i in range(4):
        row = sew([rows(m, i * 4 + j) for j in range(4)])
        for j in range(4):
            if i in (1, 2):
                put(r, i * 4 + j, 1.0 / row[j])
            else:
                put(r, i * 4 + j, row[j])
                if j > 0:
                    put(ta if i == 3 else tb, 12 + j - 1, row[j])
    stage_a(sg, (us, vs, ws, gs), p, m, r, (u, v, w, g), ta, tb)
    copies[7].wait()


def k_b(first, *refs):
    if first:
        u, v, w, g, m, r, ta, ra, tb, f3, bm, r3 = refs
        own, got = three(ta, 12), three(ra, 12)
        for j in range(4):
            put(r3, j, 1.0 / (own[j] + got[j]))
        rr = lambda j: rows(r3, j)
    else:
        u, v, w, g, m, r, ta, ra, tb, f3, bm = refs
        rr = lambda j: rows(r, 12 + j)
    _, sg = place()
    for f, field in enumerate((u, v, w, g)):
        own, got = three(ta, f * 3), three(ra, f * 3)
        for j in range(4):
            put(f3, f * 4 + j, rows(field, 12 + j) + rr(j) * (own[j] + got[j]))
    known = []
    for j in range(4):
        along = lin(D[0], [rows(u, j), rows(u, 4 + j), rows(u, 8 + j), rows(f3, j)])
        across = dy(functools.partial(rows, v), 0, j)
        known.append(rows(m, j) * (sg * along + across))
    known = sew(known)
    for j in range(1, 4):
        put(bm, 11 + j, known[j])
    for k in range(12):
        put(bm, k, rows(tb, k))
    if first:
        for j in range(4):
            put(bm, 15 + j, rows(m, j))


def k_c(first, *refs):
    if first:
        u, v, w, g, p, m, r, r3, f3, tb, rb, uo, vo, wo, go, po, dm, ro, mo = refs
        own, got = three(tb, 12), sew([rows(rb, 15 + j) for j in range(4)])
        for j in range(4):
            put(ro, j, 1.0 / (own[j] + got[j]))
            put(ro, 12 + j, rows(r3, j))
            put(mo, j, rows(rb, 15 + j))
            for i in (1, 2):
                put(ro, i * 4 + j, rows(r, i * 4 + j))
        r, mn = ro, mo
    else:
        u, v, w, g, p, m, r, mn, f3, tb, rb, uo, vo, wo, go, po, dm = refs
    _, sg = place()
    inc = []
    for f, (field, out) in enumerate(((u, uo), (v, vo), (w, wo), (g, go))):
        own, got = three(tb, f * 3), three(rb, f * 3)
        part = []
        for j in range(4):
            add = rows(r, j) * (own[j] + got[j])
            part.append(add)
            put(out, j, rows(field, j) + add)
            put(out, 12 + j, rows(f3, f * 4 + j))
            for i in (1, 2):
                put(out, i * 4 + j, rows(field, i * 4 + j))
        if f < 2:
            inc.append(part)
    other = []
    for j in range(4):
        other.append(rows(mn, j) * (lin(D[j], inc[1]) - (sg * D[0][0]) * inc[0][j]))
    other = [-SPEED * (a + b) for a, b in zip(sew(other), three(rb, 12))]
    gu, gv = functools.partial(rows, uo), functools.partial(rows, vo)
    for i in range(4):
        row = sew([rows(m, i * 4 + j) * (-SPEED * (sg * dx(gu, i, j) + dy(gv, i, j))) for j in range(4)])
        for j in range(4):
            n = i * 4 + j
            total = row[j] + other[j] if i == 0 else row[j]
            put(po, n, rows(p, n) + rows(r, n) * total)
            if i == 3 and j > 0:
                put(dm, j - 1, row[j])


def level(ref, k):
    return jnp.concatenate([ref[pl.ds(k, 8, stride=32), :], ref[pl.ds(16 + k, 8, stride=32), :]], 0)


def node_of(ref, n):
    return ref[pl.ds((n % 2) * 8 + n // 2, NL, stride=16), :]


def k_d(p, w, r, rd, wu, pu, wd, pd, edge, po, vm):
    me = lax.axis_index("lev")
    got = three(rd, 0)
    for n in range(12):
        put(po, n, rows(p, n))
    for j in range(4):
        put(po, 12 + j, rows(p, 12 + j) + rows(r, 12 + j) * got[j])
    su = sd = None
    for k in range(NL):
        wk, pk = level(w, k), level(po, k)
        a = rows(wu, k) * wk + rows(pu, k) * pk
        b = rows(wd, k) * wk + rows(pd, k) * pk
        su = a if su is None else su + a
        sd = b if sd is None else sd + b
    low, high = level(po, 0), level(po, NL - 1)
    su_far = su + rows(edge, 6) * high
    sd_far = sd - rows(edge, 5) * low
    for k, c in enumerate(ORDER):
        above = c > me
        total = jnp.where(above, jnp.where(c > me + 1, su_far, su), jnp.where(c < me - 1, sd_far, sd))
        vm[k * 32 : k * 32 + 16, :] = total
        vm[k * 32 + 16 : k * 32 + 32, :] = jnp.where(above, high, low)


def solve(p, w, rv, ia, hr, rh, cp, edge, s_out, p_out):
    me = lax.axis_index("lev")
    low, high = level(p, 0), level(p, NL - 1)
    from_below = from_above = prev = then = jnp.zeros_like(low)
    for k, c in enumerate(ORDER):
        part, side = rows(rv, 2 * k), rows(rv, 2 * k + 1)
        from_below = from_below + jnp.where(c < me, part, 0.0)
        from_above = from_above + jnp.where(c > me, part, 0.0)
        prev = jnp.where(c == me - 1, side, prev)
        then = jnp.where(c == me + 1, side, then)
    from_below = from_below * rows(edge, 7) - rows(edge, 0) * low
    from_above = from_above * rows(edge, 8) + rows(edge, 1) * high
    d = []
    last = from_below
    for k in range(NL):
        below = level(p, k - 1) if k > 0 else prev
        above = level(p, k + 1) if k < NL - 1 else then
        q = level(w, k) * rows(ia, k) - (above - below) * rows(hr, k)
        last = rows(cp, k) * (q + last)
        d.append(last)
    s = (d[NL - 1] + rows(cp, NL - 1) * from_above) * rows(edge, 2)
    after = from_above + rows(edge, 4) * s
    for k in range(NL - 1, -1, -1):
        put(s_out, k, s)
        if k > 0:
            nxt = d[k - 1] + rows(cp, k - 1) * s
        else:
            nxt = from_below + rows(edge, 3) * s
        put(p_out, k, level(p, k) - rows(rh, k) * (after - nxt))
        after, s = s, nxt


def k_e(p, w, g, u, v, rv, ia, hr, rh, cp, edge, m, r, uo, vo, wo, go, po, ta, tb, ss, ps, ws, gs):
    _, sg = place()
    solve(p, w, rv, ia, hr, rh, cp, edge, ss, ps)
    for n in range(16):
        s = node_of(ss, n)
        put(ws, n, s)
        put(gs, n, rows(g, n) + RATE * s)
        put(po, n, node_of(ps, n))
    stage_a(sg, (u, v, ws, gs), po, m, r, (uo, vo, wo, go), ta, tb)


def k_out(order, p, w, g, u, v, rv, ia, hr, rh, cp, edge, uo, vo, wo, po, go, ss, ps, us, vs, ws, qs, gs, order_s, sem):
    core, _ = place()
    (copy,) = fetch((order,), (order_s,), sem)
    copy.wait()
    index = jnp.broadcast_to(order_s[...], (NL, LANES))

    def store(value_of, held, out, k):
        for n in range(16):
            start = jnp.where(core == 1, (3 - n // 4) * 4 + n % 4, n)
            held[pl.ds(start, NL, stride=16), :] = pick(value_of(n), index)
        copy = pltpu.make_async_copy(held, out, sem.at[k])
        copy.start()
        return copy

    copies = [
        store(functools.partial(rows, u), us, uo, 1),
        store(functools.partial(rows, v), vs, vo, 2),
    ]
    solve(p, w, rv, ia, hr, rh, cp, edge, ss, ps)
    copies += [
        store(functools.partial(node_of, ss), ws, wo, 3),
        store(functools.partial(node_of, ps), qs, po, 4),
        store(lambda n: rows(g, n) + RATE * node_of(ss, n), gs, go, 5),
    ]
    for copy in copies:
        copy.wait()


def k_col(after, st, index, out, a_s, ia_s):
    index = jnp.broadcast_to(index[...], (NL, LANES))
    for k in range(16):
        a = pick(st[k * 16 : k * 16 + 16, :], index)
        a_s[k * 16 : k * 16 + 16, :] = a
        ia_s[k * 16 : k * 16 + 16, :] = 1.0 / a
    one = jnp.ones((2, LANES), F32)
    zero = jnp.zeros((2, LANES), F32)
    pair = lambda ref, k: ref[2 * k : 2 * k + 2, :]
    th, de = one, one
    below, rho = [one], [one]
    for k in range(128):
        de = de + th * pair(ia_s, k)
        th = th + de
        if k % 16 == 15:
            below.append(th)
            rho.append(de / th)
    ps, de = one, one
    above, sig = [one] * 9, [one] * 9
    for k in range(127, -1, -1):
        de = de + ps * pair(ia_s, k)
        ps = ps + de
        if k % 16 == 0:
            above[k // 16] = ps
            sig[k // 16] = de / ps
    half = lambda k: 0.5 * jnp.sqrt(pair(ia_s, k)) if 0 <= k < 128 else zero
    for place_of, b in enumerate(ORDER):
        tail = [rho[b], sig[b + 1], half(16 * b - 1), half(16 * b + 16), below[b], above[b + 1], zero, zero]
        for t in range(ROWS):
            start = (place_of * ROWS + t) * 2
            out[start : start + 2, :] = pair(a_s, b * 16 + t) if t < 16 else tail[t - 16]


def k_stat(got, after, ia, hr, rh, cp, wu, pu, wd, pd, edge, scr, tu_s, td_s):
    core, _ = place()
    size = 2 * ROWS
    for k, src in enumerate(ORDER):
        goal = jnp.where(core == 1, src ^ 6, src)
        scr[pl.ds(pl.multiple_of(goal * size, 8), size), :] = got[k * size : (k + 1) * size, :]

    def row(t):
        return jnp.concatenate([scr[pl.ds(2 * t + e, 8, stride=2 * ROWS), :] for e in range(2)], 0)

    for k in range(NL):
        a = row(k)
        ra = 1.0 / a
        root = jnp.sqrt(a)
        put(ia, k, ra)
        put(rh, k, 0.5 * root)
        put(hr, k, 0.5 * (ra * root))
    rho, sig, h_lo, h_hi, th0, ps0 = (row(16 + t) for t in range(6))
    th, de = th0, rho * th0
    for k in range(NL):
        de = de + th * rows(ia, k)
        new = th + de
        put(cp, k, th / new)
        put(tu_s, k, th)
        th = new
    ps, de = ps0, sig * ps0
    for k in range(NL - 1, -1, -1):
        de = de + ps * rows(ia, k)
        put(td_s, k, ps)
        ps = ps + de
    cpm, cqp = 1.0 - rho, 1.0 - sig
    for ref, wt, pt, in ((tu_s, wu, pu), (td_s, wd, pd)):
        for k in range(NL):
            put(wt, k, rows(ref, k) * rows(ia, k))
            value = None
            if k < NL - 1:
                value = rows(ref, k + 1) * rows(hr, k + 1)
            elif ref is td_s:
                value = rows(ref, k) * cqp * h_hi
            else:
                value = jnp.zeros_like(rho)
            if k > 0:
                value = value - rows(ref, k - 1) * rows(hr, k - 1)
            elif ref is tu_s:
                value = value - rows(ref, 0) * cpm * h_lo
            put(pt, k, value)
    put(edge, 0, cpm * h_lo)
    put(edge, 1, cqp * h_hi)
    put(edge, 2, 1.0 / (1.0 - rows(cp, NL - 1) * cqp))
    put(edge, 3, cpm)
    put(edge, 4, cqp)
    put(edge, 5, ps * h_lo)
    put(edge, 6, th * h_hi)
    put(edge, 7, 1.0 / th0)
    put(edge, 8, 1.0 / ps0)


def call(kernel, name, args, outs, scratch=(), hbm_in=0, free_out=False):
    vmem = pl.BlockSpec(memory_space=pltpu.VMEM)
    hbm = pl.BlockSpec(memory_space=pl.ANY)
    args = [
        pltpu.with_memory_space_constraint(x, pltpu.HBM if k < hbm_in else pltpu.VMEM)
        for k, x in enumerate(args)
    ]
    kind = jax.ShapeDtypeStruct if free_out else pltpu.VMEM
    spare = [pltpu.VMEM((n * NL, LANES), F32) for n in scratch]
    if hbm_in:
        spare += [pltpu.VMEM((1, LANES), jnp.int32), pltpu.SemaphoreType.DMA((8,))]
    return pl.pallas_call(
        kernel,
        out_shape=[kind((n * NL, LANES), F32) if n else kind((1, LANES), jnp.int32) for n in outs],
        in_specs=[hbm if k < hbm_in else vmem for k in range(len(args))],
        out_specs=[hbm if free_out else vmem] * len(outs),
        scratch_shapes=spare,
        compiler_params=pltpu.CompilerParams(vmem_limit_bytes=8 << 20),
        name=name,
    )(*args)


def body(zonal, meridional, vertical, pressure, geopotential, layer_mass, stiffness, order):
    count = lax.axis_size("elem")
    mates = [(i, i ^ 1) for i in range(count)]
    others = [(i, (i + 1) % count if i % 2 else (i - 1) % count) for i in range(count)]
    flat = lambda x: x.reshape(-1, LANES)
    u, v, w, p, g, lm = (flat(x) for x in (zonal, meridional, vertical, pressure, geopotential, layer_mass))

    def swap_levels(x):
        return lax.all_to_all(x.reshape(8, -1, LANES), "lev", 0, 0, tiled=True, axis_index_groups=[list(ORDER)]).reshape(-1, LANES)

    u, v, w, g, p, m, r, ta, tb, st, index = call(
        k_init, "init", [order, p, lm, u, v, w, g, flat(stiffness)], [16] * 7 + [15, 15, 16, 0], [16] * 10, hbm_in=8
    )
    mn = r3 = None
    statics = None
    for step in range(SUBSTEPS):
        first = step == 0
        ra = lax.ppermute(ta, "elem", mates)
        if first:
            f3, bm, r3 = call(functools.partial(k_b, True), "b1", [u, v, w, g, m, r, ta, ra, tb], [16, 19, 4])
        else:
            f3, bm = call(functools.partial(k_b, False), "b", [u, v, w, g, m, r, ta, ra, tb], [16, 15])
        rb = lax.ppermute(bm, "elem", others)
        if first:
            (sent,) = call(k_col, "col", [bm, st, index], [ROWS], [16, 16])
            got = swap_levels(sent)
        if first:
            u, v, w, g, p, dm, r, mn = call(
                functools.partial(k_c, True),
                "c1",
                [u, v, w, g, p, m, r, r3, f3, tb, rb],
                [16] * 5 + [LONG, 16, 4],
            )
        else:
            u, v, w, g, p, dm = call(
                functools.partial(k_c, False), "c", [u, v, w, g, p, m, r, mn, f3, tb, rb], [16] * 5 + [3]
            )
        rd = lax.ppermute(dm, "elem", mates)
        if first:
            ia, hr, rh, cp, wu, pu, wd, pd, edge = call(
                k_stat, "stat", [got, rd], [16] * 8 + [9], [ROWS, 16, 16]
            )
            statics = [ia, hr, rh, cp, edge]
        p, vm = call(k_d, "d", [p, w, r, rd, wu, pu, wd, pd, edge], [16, 16])
        rv = swap_levels(vm)
        if step < SUBSTEPS - 1:
            u, v, w, g, p, ta, tb = call(
                k_e, "e", [p, w, g, u, v, rv] + statics + [m, r], [16] * 5 + [12, 12], [16] * 4
            )
        else:
            outs = call(k_out, "out", [order, p, w, g, u, v, rv] + statics, [16] * 5, [16] * 7, hbm_in=1, free_out=True)
    return tuple(x.reshape(zonal.shape) for x in outs)


def solution(mesh):
    fields = P("lev", None, "elem")
    return jax.shard_map(
        body,
        mesh=mesh,
        in_specs=(fields,) * 6 + (P(None, "lev", "elem"), P("elem", None)),
        out_specs=(fields,) * 5,
        check_vma=False,
    )
```

```python
import functools
import math

import jax
import jax.numpy as jnp
import numpy as np
from jax import lax
from jax.experimental import pallas as pl
from jax.experimental.pallas import tpu as pltpu
from jax.sharding import PartitionSpec as P

SUBSTEPS = 3
SPEED = 0.12
DRIFT1 = 0.1
DRIFT2 = 0.06
RATE = 2.0
F32 = jnp.float32
LANES = 128
NL = 16
ORDER = (4, 0, 7, 1, 6, 2, 5, 3)
LONG = 72
ROWS = 24


def tables():
    points = np.array([-1.0, -1.0 / math.sqrt(5.0), 1.0 / math.sqrt(5.0), 1.0])
    quad = [1.0 / 6.0, 5.0 / 6.0, 5.0 / 6.0, 1.0 / 6.0]
    d = np.zeros((4, 4))
    for t in range(4):
        for s in range(4):
            if t == s:
                d[t, s] = sum(1.0 / (points[t] - points[o]) for o in range(4) if o != t)
            else:
                top = math.prod(points[t] - points[o] for o in range(4) if o != t)
                low = math.prod(points[s] - points[o] for o in range(4) if o != s)
                d[t, s] = top / (low * (points[t] - points[s]))
    d[np.abs(d) < 1e-12] = 0.0
    return [[float(x) for x in row] for row in d], [float(a * b) for a in quad for b in quad]


D, WEIGHT = tables()


def lin(coeffs, values):
    total = None
    for c, v in zip(coeffs, values):
        if c != 0.0:
            total = c * v if total is None else total + c * v
    return total


def up(x):
    return pltpu.roll(x, LANES - 1, 1)


def down(x):
    return pltpu.roll(x, 1, 1)


def sew(row):
    last = row[3] + up(row[0])
    return [down(last), row[1], row[2], last]


def rows(ref, n):
    return ref[n * NL : (n + 1) * NL, :]


def put(ref, n, value):
    ref[n * NL : (n + 1) * NL, :] = value


def dx(get, i, j):
    return lin(D[i], [get(k * 4 + j) for k in range(4)])


def dy(get, i, j):
    return lin(D[j], [get(i * 4 + k) for k in range(4)])


def three(ref, base):
    a, b, c = (rows(ref, base + k) for k in range(3))
    return [down(c), a, b, c]


def place():
    core = lax.rem(lax.axis_index("elem"), 2)
    return core, (1 - 2 * core).astype(F32)


def inverse_of(order_ref):
    order = order_ref[...].astype(F32)
    across = jnp.broadcast_to(order, (LANES, LANES))
    along = across.T
    lane = lax.broadcasted_iota(jnp.int32, (LANES, LANES), 1).astype(F32)
    slot = lax.broadcasted_iota(jnp.int32, (LANES, LANES), 0).astype(F32)
    return jnp.sum(jnp.where(along == lane, slot, 0.0), axis=0, keepdims=True).astype(jnp.int32)


def pick(values, index):
    return jnp.take_along_axis(values, index, axis=1, mode="promise_in_bounds")


def stage_a(sg, src, p, m, r, dst, ta, tb, own_face):
    for f in range(4):
        if f < 2:
            get = functools.partial(rows, p)
        else:
            get = functools.partial(rows, src[f])
        for i in (3,) if own_face else (0, 1, 2):
            row = []
            for j in range(4):
                if f == 0:
                    t = (-SPEED * sg) * dx(get, i, j)
                elif f == 1:
                    t = -SPEED * dy(get, i, j)
                else:
                    t = -((DRIFT1 * sg) * dx(get, i, j) + DRIFT2 * dy(get, i, j))
                row.append(rows(m, i * 4 + j) * t)
            row = sew(row)
            for j in range(4):
                n = i * 4 + j
                own = rows(src[f], n)
                if i in (1, 2):
                    put(dst[f], n, own + rows(r, n) * row[j])
                elif j > 0:
                    put(ta if i == 3 else tb, f * 3 + j - 1, row[j])
                if i == 0:
                    put(dst[f], n, own)
                    put(dst[f], 12 + j, rows(src[f], 12 + j))


def fetch(sources, targets, sem):
    copies = [pltpu.make_async_copy(a, b, sem.at[k]) for k, (a, b) in enumerate(zip(sources, targets))]
    for copy in copies:
        copy.start()
    return copies


def k_init(order, *refs):
    ins, (us, vs, ws, gs, p, m, r, ta, st, index_out) = refs[:7], refs[7:17]
    order_s, sem = refs[23:]
    held = refs[17:23]
    copies = fetch((order,) + ins, (order_s,) + held + (st,), sem)
    core, sg = place()
    copies[0].wait()
    inverse = inverse_of(order_s)
    index_out[...] = inverse
    index = jnp.broadcast_to(inverse, (NL, LANES))
    for copy, src, dst in zip(copies[1:7], held, (p, m, us, vs, ws, gs)):
        copy.wait()
        for i in range(4):
            for j in range(4):
                start = jnp.where(core == 1, (3 - i) * 4 + j, i * 4 + j)
                value = pick(src[pl.ds(start, NL, stride=16), :], index)
                if dst is m:
                    value = value * WEIGHT[i * 4 + j]
                put(dst, i * 4 + j, value)
    for i in range(4):
        row = sew([rows(m, i * 4 + j) for j in range(4)])
        for j in range(4):
            if i in (1, 2):
                put(r, i * 4 + j, 1.0 / row[j])
            else:
                put(r, i * 4 + j, row[j])
                if i == 3 and j > 0:
                    put(ta, 12 + j - 1, row[j])
    stage_a(sg, (us, vs, ws, gs), p, m, r, None, ta, None, True)
    copies[7].wait()


def k_rest(first, us, vs, ws, gs, p, m, r, u, v, w, g, tb):
    _, sg = place()
    stage_a(sg, (us, vs, ws, gs), p, m, r, (u, v, w, g), None, tb, False)
    if first:
        for j in range(1, 4):
            put(tb, 11 + j, rows(r, j))


def k_b(first, *refs):
    if first:
        u, v, w, g, m, r, ta, ra, tb, f3, bm, r3 = refs
        own, got = three(ta, 12), three(ra, 12)
        for j in range(4):
            put(r3, j, 1.0 / (own[j] + got[j]))
        rr = lambda j: rows(r3, j)
    else:
        u, v, w, g, m, r, ta, ra, tb, f3, bm = refs
        rr = lambda j: rows(r, 12 + j)
    _, sg = place()
    for f, field in enumerate((u, v, w, g)):
        own, got = three(ta, f * 3), three(ra, f * 3)
        for j in range(4):
            put(f3, f * 4 + j, rows(field, 12 + j) + rr(j) * (own[j] + got[j]))
    known = []
    for j in range(4):
        along = lin(D[0], [rows(u, j), rows(u, 4 + j), rows(u, 8 + j), rows(f3, j)])
        across = dy(functools.partial(rows, v), 0, j)
        known.append(rows(m, j) * (sg * along + across))
    known = sew(known)
    for j in range(1, 4):
        put(bm, 11 + j, known[j])
    for k in range(12):
        put(bm, k, rows(tb, k))
    if first:
        for j in range(4):
            put(bm, 15 + j, rows(m, j))


def k_c(first, *refs):
    if first:
        u, v, w, g, p, m, r, r3, f3, tb, rb, uo, vo, wo, go, po, dm, ro, mo = refs
        own, got = three(tb, 12), sew([rows(rb, 15 + j) for j in range(4)])
        for j in range(4):
            put(ro, j, 1.0 / (own[j] + got[j]))
            put(ro, 12 + j, rows(r3, j))
            put(mo, j, rows(rb, 15 + j))
            for i in (1, 2):
                put(ro, i * 4 + j, rows(r, i * 4 + j))
        r, mn = ro, mo
    else:
        u, v, w, g, p, m, r, mn, f3, tb, rb, uo, vo, wo, go, po, dm = refs
    _, sg = place()
    inc = []
    for f, (field, out) in enumerate(((u, uo), (v, vo), (w, wo), (g, go))):
        own, got = three(tb, f * 3), three(rb, f * 3)
        part = []
        for j in range(4):
            add = rows(r, j) * (own[j] + got[j])
            part.append(add)
            put(out, j, rows(field, j) + add)
            put(out, 12 + j, rows(f3, f * 4 + j))
            for i in (1, 2):
                put(out, i * 4 + j, rows(field, i * 4 + j))
        if f < 2:
            inc.append(part)
    other = []
    for j in range(4):
        other.append(rows(mn, j) * (lin(D[j], inc[1]) - (sg * D[0][0]) * inc[0][j]))
    other = [-SPEED * (a + b) for a, b in zip(sew(other), three(rb, 12))]
    gu, gv = functools.partial(rows, uo), functools.partial(rows, vo)
    for i in range(4):
        row = sew([rows(m, i * 4 + j) * (-SPEED * (sg * dx(gu, i, j) + dy(gv, i, j))) for j in range(4)])
        for j in range(4):
            n = i * 4 + j
            total = row[j] + other[j] if i == 0 else row[j]
            put(po, n, rows(p, n) + rows(r, n) * total)
            if i == 3 and j > 0:
                put(dm, j - 1, row[j])


def level(ref, k):
    return jnp.concatenate([ref[pl.ds(k, 8, stride=32), :], ref[pl.ds(16 + k, 8, stride=32), :]], 0)


def node_of(ref, n):
    return ref[pl.ds((n % 2) * 8 + n // 2, NL, stride=16), :]


def k_d(p, w, r, rd, wu, pu, wd, pd, edge, po, vm):
    me = lax.axis_index("lev")
    got = three(rd, 0)
    for n in range(12):
        put(po, n, rows(p, n))
    for j in range(4):
        put(po, 12 + j, rows(p, 12 + j) + rows(r, 12 + j) * got[j])
    su = sd = None
    for k in range(NL):
        wk, pk = level(w, k), level(po, k)
        a = rows(wu, k) * wk + rows(pu, k) * pk
        b = rows(wd, k) * wk + rows(pd, k) * pk
        su = a if su is None else su + a
        sd = b if sd is None else sd + b
    low, high = level(po, 0), level(po, NL - 1)
    su_far = su + rows(edge, 6) * high
    sd_far = sd - rows(edge, 5) * low
    for k, c in enumerate(ORDER):
        above = c > me
        total = jnp.where(above, jnp.where(c > me + 1, su_far, su), jnp.where(c < me - 1, sd_far, sd))
        vm[k * 32 : k * 32 + 16, :] = total
        vm[k * 32 + 16 : k * 32 + 32, :] = jnp.where(above, high, low)


def solve(p, w, rv, ia, hr, rh, cp, edge, s_out, p_out):
    me = lax.axis_index("lev")
    low, high = level(p, 0), level(p, NL - 1)
    from_below = from_above = prev = then = jnp.zeros_like(low)
    for k, c in enumerate(ORDER):
        part, side = rows(rv, 2 * k), rows(rv, 2 * k + 1)
        from_below = from_below + jnp.where(c < me, part, 0.0)
        from_above = from_above + jnp.where(c > me, part, 0.0)
        prev = jnp.where(c == me - 1, side, prev)
        then = jnp.where(c == me + 1, side, then)
    from_below = from_below * rows(edge, 7) - rows(edge, 0) * low
    from_above = from_above * rows(edge, 8) + rows(edge, 1) * high
    d = []
    last = from_below
    for k in range(NL):
        below = level(p, k - 1) if k > 0 else prev
        above = level(p, k + 1) if k < NL - 1 else then
        q = level(w, k) * rows(ia, k) - (above - below) * rows(hr, k)
        last = rows(cp, k) * (q + last)
        d.append(last)
    s = (d[NL - 1] + rows(cp, NL - 1) * from_above) * rows(edge, 2)
    after = from_above + rows(edge, 4) * s
    for k in range(NL - 1, -1, -1):
        put(s_out, k, s)
        if k > 0:
            nxt = d[k - 1] + rows(cp, k - 1) * s
        else:
            nxt = from_below + rows(edge, 3) * s
        put(p_out, k, level(p, k) - rows(rh, k) * (after - nxt))
        after, s = s, nxt


def k_e(p, w, g, u, v, rv, ia, hr, rh, cp, edge, m, r, ws, gs, po, ta, ss, ps):
    _, sg = place()
    solve(p, w, rv, ia, hr, rh, cp, edge, ss, ps)
    for n in range(16):
        s = node_of(ss, n)
        put(ws, n, s)
        put(gs, n, rows(g, n) + RATE * s)
        put(po, n, node_of(ps, n))
    stage_a(sg, (u, v, ws, gs), po, m, r, None, ta, None, True)


def k_out(order, p, w, g, u, v, rv, ia, hr, rh, cp, edge, uo, vo, wo, po, go, ss, ps, us, vs, ws, qs, gs, order_s, sem):
    core, _ = place()
    (copy,) = fetch((order,), (order_s,), sem)
    copy.wait()
    index = jnp.broadcast_to(order_s[...], (NL, LANES))

    def store(value_of, held, out, k):
        for n in range(16):
            start = jnp.where(core == 1, (3 - n // 4) * 4 + n % 4, n)
            held[pl.ds(start, NL, stride=16), :] = pick(value_of(n), index)
        copy = pltpu.make_async_copy(held, out, sem.at[k])
        copy.start()
        return copy

    copies = [
        store(functools.partial(rows, u), us, uo, 1),
        store(functools.partial(rows, v), vs, vo, 2),
    ]
    solve(p, w, rv, ia, hr, rh, cp, edge, ss, ps)
    copies += [
        store(functools.partial(node_of, ss), ws, wo, 3),
        store(functools.partial(node_of, ps), qs, po, 4),
        store(lambda n: rows(g, n) + RATE * node_of(ss, n), gs, go, 5),
    ]
    for copy in copies:
        copy.wait()


def k_col(after, st, index, out, a_s, ia_s):
    index = jnp.broadcast_to(index[...], (NL, LANES))
    for k in range(16):
        a = pick(st[k * 16 : k * 16 + 16, :], index)
        a_s[k * 16 : k * 16 + 16, :] = a
        ia_s[k * 16 : k * 16 + 16, :] = 1.0 / a
    one = jnp.ones((2, LANES), F32)
    zero = jnp.zeros((2, LANES), F32)
    pair = lambda ref, k: ref[2 * k : 2 * k + 2, :]
    th, de = one, one
    below, rho = [one], [one]
    for k in range(128):
        de = de + th * pair(ia_s, k)
        th = th + de
        if k % 16 == 15:
            below.append(th)
            rho.append(de / th)
    ps, de = one, one
    above, sig = [one] * 9, [one] * 9
    for k in range(127, -1, -1):
        de = de + ps * pair(ia_s, k)
        ps = ps + de
        if k % 16 == 0:
            above[k // 16] = ps
            sig[k // 16] = de / ps
    half = lambda k: 0.5 * jnp.sqrt(pair(ia_s, k)) if 0 <= k < 128 else zero
    for place_of, b in enumerate(ORDER):
        tail = [rho[b], sig[b + 1], half(16 * b - 1), half(16 * b + 16), below[b], above[b + 1], zero, zero]
        for t in range(ROWS):
            start = (place_of * ROWS + t) * 2
            out[start : start + 2, :] = pair(a_s, b * 16 + t) if t < 16 else tail[t - 16]


def k_stat(got, after, ia, hr, rh, cp, wu, pu, wd, pd, edge, scr, tu_s, td_s):
    core, _ = place()
    size = 2 * ROWS
    for k, src in enumerate(ORDER):
        goal = jnp.where(core == 1, src ^ 6, src)
        scr[pl.ds(pl.multiple_of(goal * size, 8), size), :] = got[k * size : (k + 1) * size, :]

    def row(t):
        return jnp.concatenate([scr[pl.ds(2 * t + e, 8, stride=2 * ROWS), :] for e in range(2)], 0)

    for k in range(NL):
        a = row(k)
        ra = 1.0 / a
        root = jnp.sqrt(a)
        put(ia, k, ra)
        put(rh, k, 0.5 * root)
        put(hr, k, 0.5 * (ra * root))
    rho, sig, h_lo, h_hi, th0, ps0 = (row(16 + t) for t in range(6))
    th, de = th0, rho * th0
    for k in range(NL):
        de = de + th * rows(ia, k)
        new = th + de
        put(cp, k, th / new)
        put(tu_s, k, th)
        th = new
    ps, de = ps0, sig * ps0
    for k in range(NL - 1, -1, -1):
        de = de + ps * rows(ia, k)
        put(td_s, k, ps)
        ps = ps + de
    cpm, cqp = 1.0 - rho, 1.0 - sig
    for ref, wt, pt, in ((tu_s, wu, pu), (td_s, wd, pd)):
        for k in range(NL):
            put(wt, k, rows(ref, k) * rows(ia, k))
            value = None
            if k < NL - 1:
                value = rows(ref, k + 1) * rows(hr, k + 1)
            elif ref is td_s:
                value = rows(ref, k) * cqp * h_hi
            else:
                value = jnp.zeros_like(rho)
            if k > 0:
                value = value - rows(ref, k - 1) * rows(hr, k - 1)
            elif ref is tu_s:
                value = value - rows(ref, 0) * cpm * h_lo
            put(pt, k, value)
    put(edge, 0, cpm * h_lo)
    put(edge, 1, cqp * h_hi)
    put(edge, 2, 1.0 / (1.0 - rows(cp, NL - 1) * cqp))
    put(edge, 3, cpm)
    put(edge, 4, cqp)
    put(edge, 5, ps * h_lo)
    put(edge, 6, th * h_hi)
    put(edge, 7, 1.0 / th0)
    put(edge, 8, 1.0 / ps0)


def call(kernel, name, args, outs, scratch=(), hbm_in=0, free_out=False):
    vmem = pl.BlockSpec(memory_space=pltpu.VMEM)
    hbm = pl.BlockSpec(memory_space=pl.ANY)
    args = [
        pltpu.with_memory_space_constraint(x, pltpu.HBM if k < hbm_in else pltpu.VMEM)
        for k, x in enumerate(args)
    ]
    kind = jax.ShapeDtypeStruct if free_out else pltpu.VMEM
    spare = [pltpu.VMEM((n * NL, LANES), F32) for n in scratch]
    if hbm_in:
        spare += [pltpu.VMEM((1, LANES), jnp.int32), pltpu.SemaphoreType.DMA((8,))]
    return pl.pallas_call(
        kernel,
        out_shape=[kind((n * NL, LANES), F32) if n else kind((1, LANES), jnp.int32) for n in outs],
        in_specs=[hbm if k < hbm_in else vmem for k in range(len(args))],
        out_specs=[hbm if free_out else vmem] * len(outs),
        scratch_shapes=spare,
        compiler_params=pltpu.CompilerParams(vmem_limit_bytes=8 << 20),
        name=name,
    )(*args)


def body(zonal, meridional, vertical, pressure, geopotential, layer_mass, stiffness, order):
    count = lax.axis_size("elem")
    mates = [(i, i ^ 1) for i in range(count)]
    others = [(i, (i + 1) % count if i % 2 else (i - 1) % count) for i in range(count)]
    flat = lambda x: x.reshape(-1, LANES)
    u, v, w, p, g, lm = (flat(x) for x in (zonal, meridional, vertical, pressure, geopotential, layer_mass))

    def swap_levels(x):
        return lax.all_to_all(x.reshape(8, -1, LANES), "lev", 0, 0, tiled=True, axis_index_groups=[list(ORDER)]).reshape(-1, LANES)

    u, v, w, g, p, m, r, ta, st, index = call(
        k_init, "init", [order, p, lm, u, v, w, g, flat(stiffness)], [16] * 7 + [15, 16, 0], [16] * 6, hbm_in=8
    )
    mn = r3 = None
    statics = None
    for step in range(SUBSTEPS):
        first = step == 0
        ra = lax.ppermute(ta, "elem", mates)
        u, v, w, g, tb = call(
            functools.partial(k_rest, first), "rest", [u, v, w, g, p, m, r], [16] * 4 + [15 if first else 12]
        )
        if first:
            f3, bm, r3 = call(functools.partial(k_b, True), "b1", [u, v, w, g, m, r, ta, ra, tb], [16, 19, 4])
        else:
            f3, bm = call(functools.partial(k_b, False), "b", [u, v, w, g, m, r, ta, ra, tb], [16, 15])
        rb = lax.ppermute(bm, "elem", others)
        if first:
            (sent,) = call(k_col, "col", [bm, st, index], [ROWS], [16, 16])
            got = swap_levels(sent)
        if first:
            u, v, w, g, p, dm, r, mn = call(
                functools.partial(k_c, True),
                "c1",
                [u, v, w, g, p, m, r, r3, f3, tb, rb],
                [16] * 5 + [LONG, 16, 4],
            )
        else:
            u, v, w, g, p, dm = call(
                functools.partial(k_c, False), "c", [u, v, w, g, p, m, r, mn, f3, tb, rb], [16] * 5 + [3]
            )
        rd = lax.ppermute(dm, "elem", mates)
        if first:
            ia, hr, rh, cp, wu, pu, wd, pd, edge = call(
                k_stat, "stat", [got, rd], [16] * 8 + [9], [ROWS, 16, 16]
            )
            statics = [ia, hr, rh, cp, edge]
        p, vm = call(k_d, "d", [p, w, r, rd, wu, pu, wd, pd, edge], [16, 16])
        rv = swap_levels(vm)
        if step < SUBSTEPS - 1:
            w, g, p, ta = call(
                k_e, "e", [p, w, g, u, v, rv] + statics + [m, r], [16] * 3 + [12], [16] * 2
            )
        else:
            outs = call(k_out, "out", [order, p, w, g, u, v, rv] + statics, [16] * 5, [16] * 7, hbm_in=1, free_out=True)
    return tuple(x.reshape(zonal.shape) for x in outs)


def solution(mesh):
    fields = P("lev", None, "elem")
    return jax.shard_map(
        body,
        mesh=mesh,
        in_specs=(fields,) * 6 + (P(None, "lev", "elem"), P("elem", None)),
        out_specs=(fields,) * 5,
        check_vma=False,
    )
```
